256 devices in a mesh: seq: 32 (over z, y), ffn: 8 (over x, core).
Axes of the slice: x: 4, y: 4, z: 8, core: 2. Of those that a mesh axis runs over, the one named last changes fastest.
Arguments:
- patches: bfloat16 [8192, 4096], P('seq'), may hold values from -100 to 100
- gate_weight: bfloat16 [4096, 7168], P('seq', 'ffn'), may hold values from -0.09375 to 0.09375
- up_weight: bfloat16 [4096, 7168], P('seq', 'ffn'), may hold values from -0.09375 to 0.09375
- down_weight: bfloat16 [4096, 7168], P('seq', 'ffn'), may hold values from -0.25 to 0.25
- key_weight: bfloat16 [4096, 1024], P(None, 'ffn'), may hold values from -0.09375 to 0.09375
- value_weight: bfloat16 [4096, 1024], P(None, 'ffn'), may hold values from -0.09375 to 0.09375
- byte_states: bfloat16 [65536, 1024], P('seq'), may hold values from -60 to 60
- byte_patch: int32 [65536], P('seq'), may hold values from 0 to 8191, as said below
- cross_query: bfloat16 [1024, 1024], P(None, 'ffn'), may hold values from -0.375 to 0.375
- self_query: bfloat16 [1024, 1024], P(None, 'ffn'), may hold values from -0.375 to 0.375
- self_key: bfloat16 [1024, 1024], P(None, 'ffn'), may hold values from -0.375 to 0.375
- self_value: bfloat16 [1024, 1024], P(None, 'ffn'), may hold values from -0.1875 to 0.1875
- cross_out: bfloat16 [1024, 1024], P('ffn'), may hold values from -0.1875 to 0.1875
- self_out: bfloat16 [1024, 1024], P('ffn'), may hold values from -0.1875 to 0.1875
Outputs:
- update: bfloat16 [65536, 1024], P('seq', 'ffn')
The draws below stay inside these ranges and needn't reach their ends.
Inputs may be any that keep to these rules, and one draw needn't show every extreme that they name: byte_patch starts at 0, never falls, rises by at most 1 from one byte to the next and ends at 8191, so every patch is a run of one or more bytes. The bytes s * 2048 to (s + 1) * 2048 - 1 read only patches s * 256 - 23 to (s + 1) * 256 + 15; both ends are reached in every draw.
All inputs are finite; a program needn't handle non-finite values.
Results may differ from the reference program's by a relative error of at most 0.0085.
The reference program's roundings to bfloat16 on the way (of `normed`, `hidden`, `global_out`, `weights_c`, `context_c`, `weights_s` and `context_s`) count: a program that leaves them out, or rounds other values in their place, can miss the bound.
Values may be sent and summed in bfloat16 or wider, within the bound.
No kernel may reach another device: no remote copies, remote signals or barrier semaphores. Data moves between devices by JAX's collectives and lax.ppermute only.
A program may use at most 128 MiB of HBM per device.

```python
import math
import jax
import jax.numpy as jnp
from jax import lax

D = 4096
FFW = 7168
DL = 1024
HD = 64
HEADS = 16
PWIN = 8
WINDOW = 512
DRIFT = 16
P_DEV = 256
B_DEV = 2048
NPATCH = 8192
NBYTES = 65536
N_SEQ = 32


def draw_patches(key, part):
    key_rows, key_cols, key_base = jax.random.split(jax.random.fold_in(key, 5), 3)
    row_scale = jnp.exp(jax.random.uniform(key_rows, (NPATCH, 1), minval=math.log(0.5), maxval=math.log(5.0)))
    col_scale = jnp.exp(jax.random.uniform(key_cols, (1, D), minval=math.log(0.2), maxval=math.log(2.0)))
    values = jnp.clip(jax.random.normal(key_base, (NPATCH, D)), -4.0, 4.0)
    return jnp.clip(values * row_scale * col_scale, -100.0, 100.0).astype(jnp.bfloat16)


def draw_byte_states(key, part):
    key_rows, key_base = jax.random.split(jax.random.fold_in(key, 7), 2)
    row_scale = jnp.exp(jax.random.uniform(key_rows, (NBYTES, 1), minval=math.log(0.5), maxval=math.log(2.0)))
    values = jnp.clip(jax.random.normal(key_base, (NBYTES, DL)), -4.0, 4.0)
    return jnp.clip(values * row_scale, -60.0, 60.0).astype(jnp.bfloat16)


def draw_byte_patch(key, part):
    key_drift, key_pick, key_score = jax.random.split(jax.random.fold_in(key, 17), 3)
    shifts = jax.random.randint(key_drift, (N_SEQ + 1,), -DRIFT, DRIFT + 1)
    chosen = jax.random.permutation(key_pick, N_SEQ - 1)[:2] + 1
    slab_ids = jnp.arange(N_SEQ + 1, dtype=jnp.int32)
    shifts = jnp.where(slab_ids == chosen[0], -DRIFT, shifts)
    shifts = jnp.where(slab_ids == chosen[1], DRIFT, shifts)
    shifts = jnp.where((slab_ids == 0) | (slab_ids == N_SEQ), 0, shifts)
    slab_start = slab_ids * B_DEV + shifts
    lengths = slab_start[1:] - slab_start[:-1]
    longest = B_DEV + 2 * DRIFT
    places = jnp.arange(1, longest, dtype=jnp.int32)
    limit = 1073741824 // longest
    scores = jax.random.randint(key_score, (N_SEQ, longest - 1), 0, limit) * longest + places[None, :]
    slab_rows = jnp.arange(N_SEQ, dtype=jnp.int32)[:, None]
    forced_low = (slab_rows == chosen[0]) & (places[None, :] <= DRIFT)
    forced_high = (slab_rows + 1 == chosen[1]) & (places[None, :] >= lengths[:, None] - DRIFT)
    scores = jnp.where(forced_low | forced_high, 1073741824 + places[None, :], scores)
    scores = jnp.where(places[None, :] < lengths[:, None], scores, -places[None, :])
    picked = lax.top_k(scores, P_DEV - 1)[1].astype(jnp.int32) + 1
    cuts = jnp.sort(picked, axis=1)
    starts = jnp.concatenate([jnp.zeros((N_SEQ, 1), jnp.int32), cuts], axis=1) + slab_start[:N_SEQ, None]
    positions = jnp.arange(NBYTES, dtype=jnp.int32)
    found = jnp.searchsorted(starts.reshape(-1), positions, side='right')
    return (found - 1).astype(jnp.int32)


def steps_of(stream_key, shape, shards, least, largest):
    loudness, own = 1.0, jax.random.fold_in(stream_key, 6)
    for axis_at, parts in shards:
        heights = jnp.exp(jax.random.uniform(jax.random.fold_in(own, axis_at), (parts,), jnp.float32, least / len(shards), largest / len(shards)))
        loudness = loudness * jnp.repeat(heights, shape[axis_at] // parts).reshape([-1 if axis == axis_at else 1 for axis in range(len(shape))])
    return loudness


def noise(stream_key, extent, deviation, most, pieces=(), kind=jnp.bfloat16):
    factor_of = steps_of(stream_key, extent, pieces, -0.22, 0.18) if pieces else 1.0
    drawn = jax.random.normal(stream_key, extent, jnp.float32) * deviation * factor_of
    return jnp.minimum(jnp.maximum(drawn, -most), most).astype(kind)


def setup_inputs(seed: int = 0) -> dict:
    seeds = jax.random.split(jax.random.key(seed), 15)
    patches = draw_patches(jax.random.fold_in(seeds[14], 71), 0)
    gate_weight = noise(seeds[1], (D, FFW), D ** -0.5, 0.09375, ((0, 32), (1, 8)))
    up_weight = noise(seeds[2], (D, FFW), D ** -0.5, 0.09375, ((0, 32), (1, 8)))
    down_weight = noise(seeds[3], (D, FFW), (FFW // 16) ** -0.5, 0.25, ((0, 32), (1, 8)))
    key_weight = noise(seeds[4], (D, DL), D ** -0.5, 0.09375, ((1, 8),))
    value_weight = noise(seeds[5], (D, DL), D ** -0.5, 0.09375, ((1, 8),))
    byte_states = draw_byte_states(jax.random.fold_in(seeds[14], 71), 0)
    byte_patch = draw_byte_patch(jax.random.fold_in(seeds[14], 71), 0)
    cross_query = noise(seeds[8], (DL, DL), (DL // 4) ** -0.5, 0.375, ((1, 8),))
    self_query = noise(seeds[9], (DL, DL), (DL // 4) ** -0.5, 0.375, ((1, 8),))
    self_key = noise(seeds[10], (DL, DL), (DL // 4) ** -0.5, 0.375, ((1, 8),))
    self_value = noise(seeds[11], (DL, DL), DL ** -0.5, 0.1875, ((1, 8),))
    cross_out = noise(seeds[12], (DL, DL), DL ** -0.5, 0.1875, ((0, 8),))
    self_out = noise(seeds[13], (DL, DL), DL ** -0.5, 0.1875, ((0, 8),))
    return {"patches": patches, "gate_weight": gate_weight, "up_weight": up_weight, "down_weight": down_weight, "key_weight": key_weight, "value_weight": value_weight, "byte_states": byte_states, "byte_patch": byte_patch, "cross_query": cross_query, "self_query": self_query, "self_key": self_key, "self_value": self_value, "cross_out": cross_out, "self_out": self_out}


EPS = 1e-05

def row_normalize(matrix):
    widened = matrix.astype(jnp.float32)
    return widened * lax.rsqrt(lax.optimization_barrier(jnp.mean(widened * widened, axis=-1, keepdims=True)) + EPS)

def masked_softmax(scores, key_mask):
    masked = jnp.where(key_mask, scores, -jnp.inf)
    row_max = lax.optimization_barrier(jnp.max(masked, axis=-1, keepdims=True))
    exp_terms = jnp.exp(masked - row_max)
    return exp_terms / lax.optimization_barrier(jnp.sum(exp_terms, axis=-1, keepdims=True))

def reference(patches, gate_weight, up_weight, down_weight, key_weight, value_weight, byte_states, byte_patch, cross_query, self_query, self_key, self_value, cross_out, self_out):
    normed = row_normalize(patches).astype(jnp.bfloat16)
    gate_sum = jnp.dot(normed, gate_weight, preferred_element_type=jnp.float32)
    up_sum = jnp.dot(normed, up_weight, preferred_element_type=jnp.float32)
    hidden = (jax.nn.silu(gate_sum) * up_sum).astype(jnp.bfloat16)
    ffn_out = lax.dot_general(hidden, down_weight, (((1,), (1,)), ((), ())), preferred_element_type=jnp.float32)
    global_out = (patches.astype(jnp.float32) + ffn_out).astype(jnp.bfloat16)
    keys_c = jnp.dot(global_out, key_weight, preferred_element_type=jnp.float32).astype(jnp.bfloat16)
    values_c = jnp.dot(global_out, value_weight, preferred_element_type=jnp.float32).astype(jnp.bfloat16)
    query_c = jnp.dot(byte_states, cross_query, preferred_element_type=jnp.float32).astype(jnp.bfloat16)
    query_s = jnp.dot(byte_states, self_query, preferred_element_type=jnp.float32).astype(jnp.bfloat16)
    keys_s = jnp.dot(byte_states, self_key, preferred_element_type=jnp.float32).astype(jnp.bfloat16)
    values_s = jnp.dot(byte_states, self_value, preferred_element_type=jnp.float32).astype(jnp.bfloat16)
    score_scale = 1.0 / math.sqrt(HD)
    key_span = WINDOW + PWIN
    blocks = NBYTES // WINDOW

    def cross_block(block_id):
        offset = (block_id * WINDOW).astype(jnp.int32)
        query_block = lax.dynamic_slice_in_dim(query_c, offset, WINDOW, 0).astype(jnp.float32).reshape(WINDOW, HEADS, HD)
        patch_block = lax.dynamic_slice_in_dim(byte_patch, offset, WINDOW, 0)
        first_key = jnp.clip(patch_block[0] - PWIN + 1, 0, NPATCH - key_span).astype(jnp.int32)
        key_block = lax.dynamic_slice_in_dim(keys_c, first_key, key_span, 0).astype(jnp.float32).reshape(key_span, HEADS, HD)
        value_block = lax.dynamic_slice_in_dim(values_c, first_key, key_span, 0).astype(jnp.float32).reshape(key_span, HEADS, HD)
        key_index = first_key + jnp.arange(key_span, dtype=jnp.int32)
        key_mask = (key_index[None, :] <= patch_block[:, None]) & (key_index[None, :] > patch_block[:, None] - PWIN)
        scores = jnp.einsum('qhd,khd->hqk', query_block, key_block) * score_scale
        weights_c = masked_softmax(scores, key_mask[None]).astype(jnp.bfloat16)
        context = jnp.einsum('hqk,khd->qhd', weights_c.astype(jnp.float32), value_block)
        return context.astype(jnp.bfloat16).reshape(WINDOW, DL)
    context_c = lax.map(cross_block, jnp.arange(blocks, dtype=jnp.int32)).reshape(NBYTES, DL)
    keys_padded = jnp.concatenate([jnp.zeros((WINDOW, DL), jnp.bfloat16), keys_s], axis=0)
    values_padded = jnp.concatenate([jnp.zeros((WINDOW, DL), jnp.bfloat16), values_s], axis=0)

    def self_block(block_id):
        offset = (block_id * WINDOW).astype(jnp.int32)
        query_block = lax.dynamic_slice_in_dim(query_s, offset, WINDOW, 0).astype(jnp.float32).reshape(WINDOW, HEADS, HD)
        key_block = lax.dynamic_slice_in_dim(keys_padded, offset, 2 * WINDOW, 0).astype(jnp.float32).reshape(2 * WINDOW, HEADS, HD)
        value_block = lax.dynamic_slice_in_dim(values_padded, offset, 2 * WINDOW, 0).astype(jnp.float32).reshape(2 * WINDOW, HEADS, HD)
        query_pos = offset + jnp.arange(WINDOW, dtype=jnp.int32)
        key_pos = offset - WINDOW + jnp.arange(2 * WINDOW, dtype=jnp.int32)
        key_mask = (key_pos[None, :] <= query_pos[:, None]) & (key_pos[None, :] > query_pos[:, None] - WINDOW) & (key_pos[None, :] >= 0)
        scores = jnp.einsum('qhd,khd->hqk', query_block, key_block) * score_scale
        weights_s = masked_softmax(scores, key_mask[None]).astype(jnp.bfloat16)
        context = jnp.einsum('hqk,khd->qhd', weights_s.astype(jnp.float32), value_block)
        return context.astype(jnp.bfloat16).reshape(WINDOW, DL)
    context_s = lax.map(self_block, jnp.arange(blocks, dtype=jnp.int32)).reshape(NBYTES, DL)
    update = jnp.dot(context_c, cross_out, preferred_element_type=jnp.float32) + jnp.dot(context_s, self_out, preferred_element_type=jnp.float32)
    return update.astype(jnp.bfloat16)
```

```python
import math

import jax
import jax.numpy as jnp
from jax import lax
from jax.sharding import Mesh, PartitionSpec as P

HD = 64
PWIN = 8
WINDOW = 512
HALO = 23
EPS = 1e-05

NZ, NY, NX, NC = 8, 4, 4, 2
NF = NX * NC
SEQ = ("z", "y")
FFN = ("x", "c")
BF = jnp.bfloat16
F32 = jnp.float32


def swap(value, axes):
    return lax.all_to_all(value, axes, split_axis=0, concat_axis=0, tiled=True)


def spread(value, axes, count):
    return swap(jnp.broadcast_to(value[None], (count,) + value.shape), axes)


def row_normalize(matrix):
    widened = matrix.astype(F32)
    return widened * lax.rsqrt(jnp.mean(widened * widened, axis=-1, keepdims=True) + EPS)


def masked_softmax(scores, key_mask):
    masked = jnp.where(key_mask, scores, -jnp.inf)
    row_max = jnp.max(masked, axis=-1, keepdims=True)
    exp_terms = jnp.exp(masked - row_max)
    return exp_terms / jnp.sum(exp_terms, axis=-1, keepdims=True)


def with_halo(value, width):
    count, length = NZ * NY, value.shape[0]
    up = [(i, i + 1) for i in range(count - 1)]
    down = [(j, i) for i, j in up]
    before = lax.ppermute(value[length - width :], SEQ, up)
    after = lax.ppermute(value[:width], SEQ, down)
    return jnp.concatenate([before, value, after], axis=0)


def local(
    patches,
    gate_weight,
    up_weight,
    down_weight,
    key_weight,
    value_weight,
    byte_states,
    byte_patch,
    cross_query,
    self_query,
    self_key,
    self_value,
    cross_out,
    self_out,
):
    y = lax.axis_index("y")
    core = lax.axis_index("c")
    seq_index = lax.axis_index(SEQ)
    rows, width = patches.shape
    d_rows, hid = gate_weight.shape
    hid_y = hid // NY
    hid_z = hid // NZ
    pad_y = -hid_y % 128
    slot = hid_y + pad_y
    head_cols = key_weight.shape[1]
    both_cols = 2 * head_cols

    def by_y(weight):
        pieces = weight.reshape(d_rows, NY, hid_y).transpose(1, 0, 2)
        return jnp.pad(pieces, ((0, 0), (0, 0), (0, pad_y)))

    gate_up = swap(jnp.concatenate([by_y(gate_weight), by_y(up_weight)], axis=2), "y")
    gate_up = lax.all_gather(gate_up.reshape(NY * d_rows, 2 * slot), "z", axis=0, tiled=True)

    normed = row_normalize(patches).astype(BF)
    half = rows // NC
    own_half = lax.dynamic_slice_in_dim(normed, core * half, half, axis=0)
    group = spread(spread(own_half, "y", NY), "c", NC)
    group = group.reshape(NC * NY * half, width)

    kv_weight = jnp.concatenate([key_weight, value_weight], axis=1)
    kv_rows = lax.dynamic_index_in_dim(
        kv_weight.reshape(NZ, NY, d_rows, both_cols), y, axis=1, keepdims=False
    ).reshape(NZ * d_rows, both_cols)
    kv_all = spread(kv_rows, FFN, NF).reshape(NF, NZ * d_rows, both_cols)
    down_t = swap(down_weight.T.reshape(NZ, hid_z, d_rows), "z")
    down_t = down_t.reshape(NZ, hid_z, d_rows).transpose(1, 0, 2).reshape(hid_z, NZ * d_rows)
    mix = jnp.einsum("hd,fdc->fhc", down_t, kv_all, preferred_element_type=F32)
    mix = swap(mix.reshape(NY, NF // NY * hid_z, both_cols), "y")
    mix = jnp.sum(mix, axis=0).astype(BF)
    mix = lax.all_gather(mix, SEQ, axis=0, tiled=True)
    mix = mix.reshape(NY, NZ // NY, NY, NF // NY, hid_z, both_cols).transpose(2, 3, 0, 1, 4, 5)
    mix = mix.reshape(NF, NY, hid_y, both_cols)
    mix = jnp.pad(mix, ((0, 0), (0, 0), (0, pad_y), (0, 0)))

    own_kv = jnp.dot(patches, kv_weight, preferred_element_type=F32)

    byte_count = byte_states.shape[0]
    head_count = head_cols // HD
    score_scale = 1.0 / math.sqrt(HD)

    def project(weight):
        return jnp.dot(byte_states, weight, preferred_element_type=F32).astype(BF)

    keys_s, values_s = project(self_key), project(self_value)
    both_s = jnp.concatenate([keys_s, values_s], axis=1)
    count = NZ * NY
    before = lax.ppermute(
        both_s[byte_count - WINDOW :], SEQ, [(i, i + 1) for i in range(count - 1)]
    )
    query_s = project(self_query)
    query_c = project(cross_query)
    stacked = jnp.concatenate([before, both_s], axis=0)
    blocks = byte_count // WINDOW
    lower_half = stacked[:byte_count].reshape(blocks, WINDOW, both_cols)
    upper_half = stacked[WINDOW:].reshape(blocks, WINDOW, both_cols)
    key_pairs = jnp.concatenate([lower_half, upper_half], axis=1)
    window_keys = key_pairs[:, :, :head_cols].reshape(blocks, 2 * WINDOW, head_count, HD)
    window_values = key_pairs[:, :, head_cols:].reshape(blocks, 2 * WINDOW, head_count, HD)
    window_queries = query_s.reshape(blocks, WINDOW, head_count, HD)
    self_scores = (
        jnp.einsum("bqhd,bkhd->bhqk", window_queries, window_keys, preferred_element_type=F32)
        * score_scale
    )
    query_slot = jnp.arange(WINDOW, dtype=jnp.int32)[:, None]
    key_slot = jnp.arange(2 * WINDOW, dtype=jnp.int32)[None, :]
    band_mask = (key_slot > query_slot) & (key_slot <= query_slot + WINDOW)
    block_ids = jnp.arange(blocks, dtype=jnp.int32)
    key_pos = (
        seq_index * byte_count
        - WINDOW
        + block_ids[:, None] * WINDOW
        + jnp.arange(2 * WINDOW, dtype=jnp.int32)[None, :]
    )
    self_mask = band_mask[None, None] & (key_pos >= 0)[:, None, None, :]
    weights_s = masked_softmax(self_scores, self_mask).astype(BF)
    context_s = jnp.einsum(
        "bhqk,bkhd->bqhd", weights_s, window_values, preferred_element_type=F32
    )
    context_s = context_s.astype(BF).reshape(NF, byte_count // NF, head_cols)
    context_s = swap(context_s, FFN)
    outs = spread(jnp.stack([cross_out, self_out]), FFN, NF)
    outs = outs.reshape(NF, 2, head_cols, NF, head_cols)
    self_part = jnp.einsum(
        "frd,fdgo->gro", context_s, outs[:, 1], preferred_element_type=F32
    )

    sums = jnp.dot(group, gate_up, preferred_element_type=F32)
    hidden = (jax.nn.silu(sums[:, :slot]) * sums[:, slot:]).astype(BF)
    hidden = hidden.reshape(NC, NY, half, slot).transpose(1, 0, 2, 3).reshape(NY, rows, slot)
    hidden = swap(hidden, "y")
    part = jnp.einsum("yrk,fykc->frc", hidden, mix, preferred_element_type=F32).astype(BF)
    part = swap(part, FFN)
    both_c = (own_kv + jnp.sum(part.astype(F32), axis=0)).astype(BF)

    extended = with_halo(both_c, HALO)
    key_count = extended.shape[0]
    key_index = seq_index * rows - HALO + jnp.arange(key_count, dtype=jnp.int32)
    cross_mask = (
        (key_index[None, :] <= byte_patch[:, None])
        & (key_index[None, :] > byte_patch[:, None] - PWIN)
        & (key_index[None, :] >= 0)
    )
    query_here = query_c.reshape(byte_count, head_count, HD)
    keys_here = extended[:, :head_cols].reshape(key_count, head_count, HD)
    values_here = extended[:, head_cols:].reshape(key_count, head_count, HD)
    cross_scores = (
        jnp.einsum("qhd,khd->hqk", query_here, keys_here, preferred_element_type=F32)
        * score_scale
    )
    weights_c = masked_softmax(cross_scores, cross_mask[None]).astype(BF)
    context_c = jnp.einsum("hqk,khd->qhd", weights_c, values_here, preferred_element_type=F32)
    context_c = context_c.astype(BF).reshape(NF, byte_count // NF, head_cols)
    context_c = swap(context_c, FFN)
    update = self_part + jnp.einsum(
        "frd,fdgo->gro", context_c, outs[:, 0], preferred_element_type=F32
    )
    return swap(update.astype(BF), FFN).reshape(byte_count, head_cols)


def solution(mesh):
    fine = Mesh(mesh.devices.reshape(NZ, NY, NX, NC), SEQ + FFN)
    placed = (
        P(SEQ, None),
        P(SEQ, FFN),
        P(SEQ, FFN),
        P(SEQ, FFN),
        P(None, FFN),
        P(None, FFN),
        P(SEQ, None),
        P(SEQ),
        P(None, FFN),
        P(None, FFN),
        P(None, FFN),
        P(None, FFN),
        P(FFN, None),
        P(FFN, None),
    )
    return jax.shard_map(
        local, mesh=fine, in_specs=placed, out_specs=P(SEQ, FFN), check_vma=False
    )
```

```python
import math

import jax
import jax.numpy as jnp
from jax import lax
from jax.experimental import pallas as pl
from jax.experimental.pallas import tpu as pltpu
from jax.sharding import Mesh, PartitionSpec as P


HD = 64
PWIN = 8
WINDOW = 512
HALO = 23
EPS = 1e-05

NZ, NY, NX, NC = 8, 4, 4, 2
NF = NX * NC
SEQ = ("z", "y")
FFN = ("x", "c")
BF = jnp.bfloat16
F32 = jnp.float32


def swap(value, axes):
    return lax.all_to_all(value, axes, split_axis=0, concat_axis=0, tiled=True)


UP = [(i, (i + 1) % 4) for i in range(4)]
DOWN = [(i, (i - 1) % 4) for i in range(4)]
ACROSS = [(i, (i + 2) % 4) for i in range(4)]


def ring(value, axis):
    half = value.shape[0] // 2
    before = lax.ppermute(value, axis, UP)
    after = lax.ppermute(value, axis, DOWN)
    far_low = lax.ppermute(before[:half], axis, UP)
    far_high = lax.ppermute(after[half:], axis, DOWN)
    return before, after, far_low, far_high


def other_core(value):
    return lax.ppermute(value, "c", [(0, 1), (1, 0)])


def in_order(own, other, x, core):
    pair = jnp.where(core == 0, jnp.stack([own, other], 1), jnp.stack([other, own], 1))
    return lax.dynamic_slice_in_dim(jnp.concatenate([pair, pair]), (NX - x) % NX, NX, axis=0)


def part_kernel(y_ref, own_ref, next_ref, before_ref, far_ref, mix_ref, out_ref):
    keep = 2 * mix_ref.shape[3]
    total = None
    for step, ref in ((0, own_ref), (1, next_ref), (3, before_ref), (2, far_ref)):
        piece = mix_ref[pl.ds(2 * ((y_ref[0] + step) % NY), 2), 0, 0]
        piece = piece.reshape(keep, piece.shape[-1])
        term = jnp.dot(ref[:, :keep], piece, preferred_element_type=F32)
        total = term if total is None else total + term
    out_ref[0] = total.astype(BF)


def part_products(y, blocks, mix):
    rows, slot = blocks[0].shape
    hid_z, cols = mix.shape[3:]
    whole = pl.BlockSpec((rows, slot), lambda i, y_ref: (0, 0))
    return pl.pallas_call(
        part_kernel,
        out_shape=jax.ShapeDtypeStruct((NF, rows, cols), BF),
        grid_spec=pltpu.PrefetchScalarGridSpec(
            num_scalar_prefetch=1,
            grid=(NF,),
            in_specs=[whole] * 4
            + [pl.BlockSpec((NZ, 1, 1, hid_z, cols), lambda i, y_ref: (0, i // 2, i % 2, 0, 0))],
            out_specs=pl.BlockSpec((1, rows, cols), lambda i, y_ref: (i, 0, 0)),
        ),
    )(y.reshape(1).astype(jnp.int32), *blocks, mix)


def row_normalize(matrix):
    widened = matrix.astype(F32)
    return widened * lax.rsqrt(jnp.mean(widened * widened, axis=-1, keepdims=True) + EPS)


def masked_softmax(scores, key_mask):
    masked = jnp.where(key_mask, scores, -jnp.inf)
    row_max = jnp.max(masked, axis=-1, keepdims=True)
    exp_terms = jnp.exp(masked - row_max)
    return exp_terms / jnp.sum(exp_terms, axis=-1, keepdims=True)


def with_halo(value, width):
    count, length = NZ * NY, value.shape[0]
    up = [(i, i + 1) for i in range(count - 1)]
    down = [(j, i) for i, j in up]
    before = lax.ppermute(value[length - width :], SEQ, up)
    after = lax.ppermute(value[:width], SEQ, down)
    return jnp.concatenate([before, value, after], axis=0)


def local(
    patches,
    gate_weight,
    up_weight,
    down_weight,
    key_weight,
    value_weight,
    byte_states,
    byte_patch,
    cross_query,
    self_query,
    self_key,
    self_value,
    cross_out,
    self_out,
):
    x = lax.axis_index("x")
    y = lax.axis_index("y")
    core = lax.axis_index("c")
    seq_index = lax.axis_index(SEQ)
    rows, width = patches.shape
    d_rows, hid = gate_weight.shape
    hid_y = hid // NY
    hid_z = hid // NZ
    pad_y = -hid_y % 128
    slot = hid_y + pad_y
    head_cols = key_weight.shape[1]
    both_cols = 2 * head_cols

    def by_y(weight):
        pieces = weight.reshape(d_rows, NY, hid_y).transpose(1, 0, 2)
        return jnp.pad(pieces, ((0, 0), (0, 0), (0, pad_y)))

    gate_up = swap(jnp.concatenate([by_y(gate_weight), by_y(up_weight)], axis=2), "y")
    gate_up = lax.all_gather(gate_up.reshape(NY * d_rows, 2 * slot), "z", axis=0, tiled=True)

    kv_weight = jnp.concatenate([key_weight, value_weight], axis=1)
    kv_rows = lax.dynamic_index_in_dim(
        kv_weight.reshape(NZ, NY, d_rows, both_cols), y, axis=1, keepdims=False
    ).reshape(NZ * d_rows, both_cols)
    before, after, far_low, far_high = ring(kv_rows, "x")
    kv_four = jnp.concatenate([kv_rows, after, far_low, far_high, before])
    kv_four = kv_four.reshape(NX, NZ * d_rows, both_cols)
    kv_other = other_core(kv_four)
    down_t = swap(down_weight.T.reshape(NZ, hid_z, d_rows), "z")
    down_t = down_t.reshape(NZ, hid_z, d_rows).transpose(1, 0, 2).reshape(hid_z, NZ * d_rows)
    mix = in_order(
        jnp.einsum("hd,fdc->fhc", down_t, kv_four, preferred_element_type=F32),
        jnp.einsum("hd,fdc->fhc", down_t, kv_other, preferred_element_type=F32),
        x,
        core,
    )
    mix = swap(mix.reshape(NY, NF // NY * hid_z, both_cols), "y")
    mix = jnp.sum(mix, axis=0).astype(BF)
    mix = lax.all_gather(mix, SEQ, axis=0, tiled=True)
    mix = mix.reshape(NZ, NY, NF // NY, hid_z, both_cols)

    normed = row_normalize(patches).astype(BF)
    half = rows // NC
    own_half = lax.dynamic_slice_in_dim(normed, core * half, half, axis=0)
    before, after, far_low, far_high = ring(own_half, "y")
    group = jnp.concatenate(
        [
            normed,
            after,
            other_core(after),
            before,
            other_core(before),
            far_low,
            far_high,
            other_core(far_low),
            other_core(far_high),
        ]
    )

    own_kv = jnp.dot(patches, kv_weight, preferred_element_type=F32)

    byte_count = byte_states.shape[0]
    head_count = head_cols // HD
    score_scale = 1.0 / math.sqrt(HD)

    def project(weight):
        return jnp.dot(byte_states, weight, preferred_element_type=F32).astype(BF)

    keys_s, values_s = project(self_key), project(self_value)
    both_s = jnp.concatenate([keys_s, values_s], axis=1)
    count = NZ * NY
    before = lax.ppermute(
        both_s[byte_count - WINDOW :], SEQ, [(i, i + 1) for i in range(count - 1)]
    )
    query_s = project(self_query)
    query_c = project(cross_query)
    stacked = jnp.concatenate([before, both_s], axis=0)
    blocks = byte_count // WINDOW
    lower_half = stacked[:byte_count].reshape(blocks, WINDOW, both_cols)
    upper_half = stacked[WINDOW:].reshape(blocks, WINDOW, both_cols)
    key_pairs = jnp.concatenate([lower_half, upper_half], axis=1)
    window_keys = key_pairs[:, :, :head_cols].reshape(blocks, 2 * WINDOW, head_count, HD)
    window_values = key_pairs[:, :, head_cols:].reshape(blocks, 2 * WINDOW, head_count, HD)
    window_queries = query_s.reshape(blocks, WINDOW, head_count, HD)
    self_scores = (
        jnp.einsum("bqhd,bkhd->bhqk", window_queries, window_keys, preferred_element_type=F32)
        * score_scale
    )
    query_slot = jnp.arange(WINDOW, dtype=jnp.int32)[:, None]
    key_slot = jnp.arange(2 * WINDOW, dtype=jnp.int32)[None, :]
    band_mask = (key_slot > query_slot) & (key_slot <= query_slot + WINDOW)
    block_ids = jnp.arange(blocks, dtype=jnp.int32)
    key_pos = (
        seq_index * byte_count
        - WINDOW
        + block_ids[:, None] * WINDOW
        + jnp.arange(2 * WINDOW, dtype=jnp.int32)[None, :]
    )
    self_mask = band_mask[None, None] & (key_pos >= 0)[:, None, None, :]
    weights_s = masked_softmax(self_scores, self_mask).astype(BF)
    context_s = jnp.einsum(
        "bhqk,bkhd->bqhd", weights_s, window_values, preferred_element_type=F32
    )
    context_s = context_s.astype(BF).reshape(NF, byte_count // NF, head_cols)
    context_s = swap(context_s, FFN)
    outs = jnp.concatenate([cross_out, self_out])
    before, after, far_low, far_high = ring(outs, "x")
    outs = jnp.concatenate([outs, after, far_low, far_high, before])
    outs = outs.reshape(NX, 2 * head_cols, NF * head_cols)
    outs = in_order(outs, other_core(outs), x, core)
    outs = outs.reshape(NF, 2, head_cols, NF, head_cols)
    self_part = jnp.einsum(
        "frd,fdgo->gro", context_s, outs[:, 1], preferred_element_type=F32
    )

    sums = jnp.dot(group, gate_up, preferred_element_type=F32)
    hidden = (jax.nn.silu(sums[:, :slot]) * sums[:, slot:]).astype(BF)
    hidden = hidden.reshape(NY, NC, half, slot)
    far = jnp.where(core == 0, hidden[1:], hidden[1:, ::-1]).reshape(NY - 1, rows, slot)
    blocks = (
        hidden[0].reshape(rows, slot),
        lax.ppermute(far[1], "y", DOWN),
        lax.ppermute(far[0], "y", UP),
        lax.ppermute(far[2], "y", ACROSS),
    )
    part = part_products(y, blocks, mix)
    part = swap(part, FFN)
    both_c = (own_kv + jnp.sum(part.astype(F32), axis=0)).astype(BF)

    extended = with_halo(both_c, HALO)
    key_count = extended.shape[0]
    key_index = seq_index * rows - HALO + jnp.arange(key_count, dtype=jnp.int32)
    cross_mask = (
        (key_index[None, :] <= byte_patch[:, None])
        & (key_index[None, :] > byte_patch[:, None] - PWIN)
        & (key_index[None, :] >= 0)
    )
    query_here = query_c.reshape(byte_count, head_count, HD)
    keys_here = extended[:, :head_cols].reshape(key_count, head_count, HD)
    values_here = extended[:, head_cols:].reshape(key_count, head_count, HD)
    cross_scores = (
        jnp.einsum("qhd,khd->hqk", query_here, keys_here, preferred_element_type=F32)
        * score_scale
    )
    weights_c = masked_softmax(cross_scores, cross_mask[None]).astype(BF)
    context_c = jnp.einsum("hqk,khd->qhd", weights_c, values_here, preferred_element_type=F32)
    context_c = context_c.astype(BF).reshape(NF, byte_count // NF, head_cols)
    context_c = swap(context_c, FFN)
    update = self_part + jnp.einsum(
        "frd,fdgo->gro", context_c, outs[:, 0], preferred_element_type=F32
    )
    return swap(update.astype(BF), FFN).reshape(byte_count, head_cols)


def solution(mesh):
    fine = Mesh(mesh.devices.reshape(NZ, NY, NX, NC), SEQ + FFN)
    placed = (
        P(SEQ, None),
        P(SEQ, FFN),
        P(SEQ, FFN),
        P(SEQ, FFN),
        P(None, FFN),
        P(None, FFN),
        P(SEQ, None),
        P(SEQ),
        P(None, FFN),
        P(None, FFN),
        P(None, FFN),
        P(None, FFN),
        P(FFN, None),
        P(FFN, None),
    )
    return jax.shard_map(
        local, mesh=fine, in_specs=placed, out_specs=P(SEQ, FFN), check_vma=False
    )
```

```python
import math

import jax
import jax.numpy as jnp
from jax import lax
from jax.experimental import pallas as pl
from jax.experimental.pallas import tpu as pltpu
from jax.sharding import Mesh, PartitionSpec as P


HD = 64
PWIN = 8
WINDOW = 512
HALO = 32
EPS = 1e-05
QROWS = 256
BROWS = 512

NZ, NY, NX, NC = 8, 4, 4, 2
NF = NX * NC
SEQ = ("z", "y")
FFN = ("x", "c")
BF = jnp.bfloat16
F32 = jnp.float32

UP = [(i, (i + 1) % 4) for i in range(4)]
DOWN = [(i, (i - 1) % 4) for i in range(4)]
ACROSS = [(i, (i + 2) % 4) for i in range(4)]
SCALE = 1.0 / math.sqrt(HD)


def sds(shape, dtype):
    return jax.ShapeDtypeStruct(shape, dtype)


def smem(*scalars):
    return jnp.stack([s.astype(jnp.int32) for s in scalars])


def cost(micros):
    return pl.CostEstimate(
        flops=int(micros * 6e8), transcendentals=0, bytes_accessed=int(micros * 2.5e6)
    )


def call(kernel, out, *args, micros=4, scalars=None, anywhere=(), scratch=()):
    offset = 0 if scalars is None else 1
    specs = [
        pl.BlockSpec(memory_space=pl.ANY if i in anywhere else pltpu.VMEM)
        for i in range(len(args))
    ]
    if offset:
        specs = [pl.BlockSpec(memory_space=pltpu.SMEM)] + specs
        args = (scalars,) + args
    return pl.pallas_call(
        kernel,
        out_shape=out,
        in_specs=specs,
        out_specs=jax.tree.map(lambda _: pl.BlockSpec(memory_space=pltpu.VMEM), out),
        scratch_shapes=list(scratch),
        cost_estimate=cost(micros),
    )(*args)


def swap(value, axes):
    return lax.all_to_all(value, axes, split_axis=0, concat_axis=0, tiled=True)


def ring(value, axis):
    half = value.shape[0] // 2
    before = lax.ppermute(value, axis, UP)
    after = lax.ppermute(value, axis, DOWN)
    far_low = lax.ppermute(before[:half], axis, UP)
    far_high = lax.ppermute(after[half:], axis, DOWN)
    return before, after, far_low, far_high


def other_core(value):
    return lax.ppermute(value, "c", [(0, 1), (1, 0)])


def dot(a, b):
    return jnp.dot(a, b, preferred_element_type=F32)


def dot_nt(a, b):
    return lax.dot_general(a, b, (((1,), (1,)), ((), ())), preferred_element_type=F32)


def norm_kernel(place, patches, down, _after, normed, half, down_t):
    wide = patches[...].astype(F32)
    mean = jnp.mean(wide * wide, axis=-1, keepdims=True)
    normed[...] = (wide * lax.rsqrt(mean + EPS)).astype(BF)
    half[...] = normed[pl.ds(pl.multiple_of(place[2] * half.shape[0], half.shape[0]), half.shape[0])]
    flipped = down[...].T
    for z in range(NZ):
        rows = down_t.shape[1]
        down_t[z] = flipped[z * rows : (z + 1) * rows]


def mix_kernel(place, down_t, *refs):
    out = refs[-1]
    x, core = place[0], place[2]
    lhs = jnp.concatenate([down_t[z] for z in range(NZ)], axis=1)
    for side in range(2):
        own, before, after, low, high = refs[5 * side : 5 * side + 5]
        at = core if side == 0 else 1 - core
        half = low.shape[0]
        out[NC * x + at] = dot(lhs, own[...])
        out[NC * ((x + 3) % NX) + at] = dot(lhs, before[...])
        out[NC * ((x + 1) % NX) + at] = dot(lhs, after[...])
        out[NC * ((x + 2) % NX) + at] = dot(lhs[:, :half], low[...]) + dot(
            lhs[:, half:], high[...]
        )


def mix_sum_kernel(terms, cross_out, self_out, mix, outs):
    total = terms[0]
    for i in range(1, NY):
        total = total + terms[i]
    total = total.astype(BF)
    for z in range(NZ):
        mix[z] = total
    rows = cross_out.shape[0]
    outs[:rows] = cross_out[...]
    outs[rows:] = self_out[...]


def project_kernel(states, w_qs, w_qc, w_k, w_v, qs, qc, kv):
    first = dot(states[...], jnp.concatenate([w_qs[...], w_qc[...]], axis=1)).astype(BF)
    cols = qs.shape[1]
    qs[...] = first[:, :cols]
    qc[...] = first[:, cols:]
    kv[...] = dot(states[...], jnp.concatenate([w_k[...], w_v[...]], axis=1)).astype(BF)


def project(states, w_qs, w_qc, w_k, w_v):
    count, width = states.shape
    cols = w_qs.shape[1]
    weight = pl.BlockSpec((width, cols), lambda i: (0, 0))
    narrow = pl.BlockSpec((BROWS, cols), lambda i: (i, 0))
    return pl.pallas_call(
        project_kernel,
        out_shape=(sds((count, cols), BF), sds((count, cols), BF), sds((count, 2 * cols), BF)),
        grid=(count // BROWS,),
        in_specs=[pl.BlockSpec((BROWS, width), lambda i: (i, 0))] + [weight] * 4,
        out_specs=(narrow, narrow, pl.BlockSpec((BROWS, 2 * cols), lambda i: (i, 0))),
        cost_estimate=cost(6),
    )(states, w_qs, w_qc, w_k, w_v)


def window_kernel(place, query, kv, before, out, stacked):
    step = pl.program_id(0)
    cols = query.shape[1]

    @pl.when(step == 0)
    def _():
        stacked[:WINDOW] = before[...]
        stacked[WINDOW:] = kv[...]

    count = kv.shape[0]
    first = WINDOW - place[3] * count - step * QROWS
    row = lax.broadcasted_iota(jnp.int32, (QROWS, QROWS), 0)
    col = lax.broadcasted_iota(jnp.int32, (QROWS, QROWS), 1)
    tiles = WINDOW // QROWS + 1
    start = pl.multiple_of(step * QROWS, QROWS)
    for head in range(cols // HD):
        lanes = slice(head * HD, (head + 1) * HD)
        q = query[:, lanes] * SCALE
        scores = []
        for t in range(tiles):
            keys = stacked[pl.ds(start + t * QROWS, QROWS), lanes]
            s = dot_nt(q, keys)
            if t == 0:
                s = jnp.where((col > row) & (col >= first), s, -jnp.inf)
            elif t < tiles - 1:
                s = jnp.where(col >= first - t * QROWS, s, -jnp.inf)
            else:
                s = jnp.where(col <= row, s, -jnp.inf)
            scores.append(s)
        s = jnp.concatenate(scores, axis=1)
        e = jnp.exp(s - jnp.max(s, axis=-1, keepdims=True))
        w = (e * (1.0 / jnp.sum(e, axis=-1, keepdims=True))).astype(BF)
        values = stacked[
            pl.ds(start, tiles * QROWS), cols + head * HD : cols + (head + 1) * HD
        ]
        out[:, lanes] = dot(w, values).astype(BF)


def window_attention(place, query, kv, before):
    count, cols = query.shape
    block = pl.BlockSpec((QROWS, cols), lambda i: (i, 0))
    return pl.pallas_call(
        window_kernel,
        out_shape=sds((count, cols), BF),
        grid=(count // QROWS,),
        in_specs=[
            pl.BlockSpec(memory_space=pltpu.SMEM),
            block,
            pl.BlockSpec(kv.shape, lambda i: (0, 0)),
            pl.BlockSpec(before.shape, lambda i: (0, 0)),
        ],
        out_specs=block,
        scratch_shapes=[pltpu.VMEM((WINDOW + count, 2 * cols), BF)],
        cost_estimate=cost(14),
    )(place, query, kv, before)


def ffn_kernel(place, *refs):
    pieces, gate_up = refs[:9], refs[9]
    outs = refs[10:14]
    rows_buf, weight_buf, sems = refs[14:]
    core = place[2]
    rows = pieces[0].shape[0]
    half, quarter = rows // 2, rows // 4
    own, other = core * half, (1 - core) * half
    starts = [0]
    for slab in (1, 2):
        starts += [slab * rows + own, slab * rows + other]
    starts += [3 * rows + own, 3 * rows + own + quarter]
    starts += [3 * rows + other, 3 * rows + other + quarter]
    weight_copy = pltpu.make_async_copy(gate_up, weight_buf, sems.at[9])
    weight_copy.start()
    copies = []
    for i, piece in enumerate(pieces):
        size = piece.shape[0]
        at = pl.multiple_of(starts[i], quarter)
        copies.append(pltpu.make_async_copy(piece, rows_buf.at[pl.ds(at, size)], sems.at[i]))
        copies[-1].start()
    slot = outs[0].shape[1]
    weight_copy.wait()
    for slab, used in enumerate(((0,), (1, 2), (3, 4), (5, 6, 7, 8))):
        for i in used:
            copies[i].wait()
        sums = dot(rows_buf[slab * rows : (slab + 1) * rows], weight_buf[...])
        gate = sums[:, :slot]
        outs[slab][...] = (gate * (1.0 / (1.0 + jnp.exp(-gate))) * sums[:, slot:]).astype(BF)


def part_kernel(place, own, after, before, far, m_own, m_after, m_before, m_low, m_high, out, hid):
    y = place[1]
    hid[y] = own[...]
    hid[(y + 1) % NY] = after[...]
    hid[(y + 3) % NY] = before[...]
    hid[(y + 2) % NY] = far[...]
    keep = 2 * m_own.shape[2]
    cols = m_own.shape[3]
    low = m_low.shape[0]

    def product(get):
        total = None
        for block in range(NY):
            piece = jnp.concatenate([get(2 * block), get(2 * block + 1)], axis=0)
            term = dot(hid[block, :, :keep], piece)
            total = term if total is None else total + term
        return total.astype(BF)

    for p in range(2):
        out[2 * y + p] = product(lambda z: m_own[z, p])
        out[2 * ((y + 1) % NY) + p] = product(lambda z: m_after[z, p])
        out[2 * ((y + 3) % NY) + p] = product(lambda z: m_before[z, p])
        out[2 * ((y + 2) % NY) + p] = product(
            lambda z: m_low[z, p] if z < low else m_high[z - low, p]
        )


def keys_kernel(parts, own, kv, head, tail):
    total = own[...]
    for i in range(NF):
        total = total + parts[i].astype(F32)
    total = total.astype(BF)
    kv[...] = total
    head[...] = total[:HALO]
    tail[...] = total[-HALO:]


def cross_kernel(place, query, byte_patch, kv, before, after, out, stacked):
    step = pl.program_id(0)
    rows, both = kv.shape
    cols = both // 2

    @pl.when(step == 0)
    def _():
        stacked[:HALO] = before[...]
        stacked[HALO : HALO + rows] = kv[...]
        stacked[HALO + rows :] = after[...]

    total = rows + 2 * HALO
    shape = (total, query.shape[0])
    index = lax.broadcasted_iota(jnp.int32, shape, 0) + (place[3] * rows - HALO)
    held = byte_patch[...]
    mask = (index <= held) & (index > held - PWIN) & (index >= 0)
    for head in range(cols // HD):
        q = query[:, head * HD : (head + 1) * HD] * SCALE
        s = dot_nt(stacked[:, head * HD : (head + 1) * HD], q)
        s = jnp.where(mask, s, -jnp.inf)
        e = jnp.exp(s - jnp.max(s, axis=0, keepdims=True))
        w = (e * (1.0 / jnp.sum(e, axis=0, keepdims=True))).astype(BF)
        values = stacked[:, cols + head * HD : cols + (head + 1) * HD]
        context = lax.dot_general(
            values, w, (((0,), (0,)), ((), ())), preferred_element_type=F32
        )
        out[:, head * HD : (head + 1) * HD] = context.T.astype(BF)


def cross_attention(place, query, byte_patch, kv, before, after):
    count, cols = query.shape
    block = pl.BlockSpec((BROWS, cols), lambda i: (i, 0))

    def whole(value):
        return pl.BlockSpec(value.shape, lambda i: (0, 0))

    return pl.pallas_call(
        cross_kernel,
        out_shape=sds((count, cols), BF),
        grid=(count // BROWS,),
        in_specs=[
            pl.BlockSpec(memory_space=pltpu.SMEM),
            block,
            pl.BlockSpec((1, BROWS), lambda i: (0, i)),
            whole(kv),
            whole(before),
            whole(after),
        ],
        out_specs=block,
        scratch_shapes=[pltpu.VMEM((kv.shape[0] + 2 * HALO, 2 * cols), BF)],
        cost_estimate=cost(6),
    )(place, query, byte_patch.reshape(1, count), kv, before, after)


def out_product(context, outs, which):
    both = outs.shape[0] // NF
    half = both // 2
    weight = jnp.concatenate(
        [outs[f * both + which * half : f * both + (which + 1) * half] for f in range(NF)], axis=0
    )
    return dot(jnp.concatenate([context[f] for f in range(NF)], axis=1), weight)


def self_part_kernel(context, outs, out):
    out[...] = out_product(context, outs, 1)


def update_kernel(context, outs, self_part, out):
    total = (self_part[...] + out_product(context, outs, 0)).astype(BF)
    cols = out.shape[2]
    for f in range(NF):
        out[f] = total[:, f * cols : (f + 1) * cols]


def local(
    patches,
    gate_weight,
    up_weight,
    down_weight,
    key_weight,
    value_weight,
    byte_states,
    byte_patch,
    cross_query,
    self_query,
    self_key,
    self_value,
    cross_out,
    self_out,
):
    x, y, core = (lax.axis_index(a) for a in ("x", "y", "c"))
    place = smem(x, y, core, lax.axis_index(SEQ))
    rows, width = patches.shape
    d_rows, hid = gate_weight.shape
    hid_y = hid // NY
    hid_z = hid // NZ
    pad_y = -hid_y % 128
    slot = hid_y + pad_y
    head_cols = key_weight.shape[1]
    both_cols = 2 * head_cols
    byte_count = byte_states.shape[0]
    chunk = byte_count // NF

    def by_y(weight):
        pieces = weight.reshape(d_rows, NY, hid_y).transpose(1, 0, 2)
        return jnp.pad(pieces, ((0, 0), (0, 0), (0, pad_y)))

    gate_up = swap(jnp.concatenate([by_y(gate_weight), by_y(up_weight)], axis=2), "y")
    gate_up = gate_up.reshape(NY * d_rows, 2 * slot)

    def of_y(weight):
        grid = weight.reshape(NZ, NY, d_rows, head_cols)
        return lax.dynamic_slice_in_dim(grid, y, 1, axis=1)

    kv_rows = jnp.concatenate([of_y(key_weight), of_y(value_weight)], axis=3)
    kv_rows = kv_rows.reshape(NZ * d_rows, both_cols)
    kv_pieces = (kv_rows,) + ring(kv_rows, "x")
    kv_others = tuple(other_core(piece) for piece in kv_pieces)

    normed, own_half, down_t = call(
        norm_kernel,
        (
            sds((rows, width), BF),
            sds((rows // NC, width), BF),
            sds((NZ, hid_z, d_rows), BF),
        ),
        patches,
        down_weight,
        gate_up,
        scalars=place,
        anywhere=(2,),
    )
    gate_up = lax.all_gather(gate_up, "z", axis=0, tiled=True)
    down_t = swap(down_t, "z")
    before, after, far_low, far_high = ring(own_half, "y")
    group = (
        normed,
        after,
        other_core(after),
        before,
        other_core(before),
        far_low,
        far_high,
        other_core(far_low),
        other_core(far_high),
    )

    mix = call(
        mix_kernel,
        sds((NF, hid_z, both_cols), F32),
        down_t,
        *kv_pieces,
        *kv_others,
        scalars=place,
    )
    mix = swap(mix.reshape(NY, NF // NY * hid_z, both_cols), "y")
    mix, outs = call(
        mix_sum_kernel,
        (
            sds((NZ, NF // NY * hid_z, both_cols), BF),
            sds((2 * head_cols, NF * head_cols), BF),
        ),
        mix,
        cross_out,
        self_out,
    )
    mix = swap(mix, "z").reshape(NZ, NF // NY, hid_z, both_cols)
    m_before, m_after, m_low, m_high = ring(mix, "y")
    outs = lax.all_gather(outs, FFN, axis=0, tiled=True)

    own_kv = dot(patches, key_weight), dot(patches, value_weight)
    own_kv = jnp.concatenate(own_kv, axis=1)

    query_s, query_c, both_s = project(byte_states, self_query, cross_query, self_key, self_value)
    steps = [(i, i + 1) for i in range(NZ * NY - 1)]
    back = [(j, i) for i, j in steps]
    tail = lax.ppermute(both_s[byte_count - WINDOW :], SEQ, steps)
    context_s = window_attention(place, query_s, both_s, tail)
    context_s = swap(context_s.reshape(NF, chunk, head_cols), FFN)
    self_part = call(self_part_kernel, sds((chunk, NF * head_cols), F32), context_s, outs)

    piece = sds((rows, slot), BF)
    h_own, h_after, h_before, h_far = call(
        ffn_kernel,
        (piece,) * 4,
        *group,
        gate_up,
        scalars=place,
        anywhere=range(10),
        scratch=(
            pltpu.VMEM((NY * rows, width), BF),
            pltpu.VMEM(gate_up.shape, BF),
            pltpu.SemaphoreType.DMA((10,)),
        ),
    )
    part = call(
        part_kernel,
        sds((NF, rows, both_cols), BF),
        h_own,
        lax.ppermute(h_before, "y", DOWN),
        lax.ppermute(h_after, "y", UP),
        lax.ppermute(h_far, "y", ACROSS),
        mix,
        m_after,
        m_before,
        m_low,
        m_high,
        scalars=place,
        scratch=(pltpu.VMEM((NY, rows, slot), BF),),
    )
    part = swap(part, FFN)
    both_c, head_rows, tail_rows = call(
        keys_kernel,
        (sds((rows, both_cols), BF),) + (sds((HALO, both_cols), BF),) * 2,
        part,
        own_kv,
    )

    context_c = cross_attention(
        place,
        query_c,
        byte_patch,
        both_c,
        lax.ppermute(tail_rows, SEQ, steps),
        lax.ppermute(head_rows, SEQ, back),
    )
    context_c = swap(context_c.reshape(NF, chunk, head_cols), FFN)
    update = call(
        update_kernel, sds((NF, chunk, head_cols), BF), context_c, outs, self_part
    )
    return swap(update, FFN).reshape(byte_count, head_cols)


def solution(mesh):
    fine = Mesh(mesh.devices.reshape(NZ, NY, NX, NC), SEQ + FFN)
    placed = (
        P(SEQ, None),
        P(SEQ, FFN),
        P(SEQ, FFN),
        P(SEQ, FFN),
        P(None, FFN),
        P(None, FFN),
        P(SEQ, None),
        P(SEQ),
        P(None, FFN),
        P(None, FFN),
        P(None, FFN),
        P(None, FFN),
        P(FFN, None),
        P(FFN, None),
    )
    return jax.shard_map(
        local, mesh=fine, in_specs=placed, out_specs=P(SEQ, FFN), check_vma=False
    )
```

```python
import functools
import math

import jax
import jax.numpy as jnp
from jax import lax
from jax.experimental import pallas as pl
from jax.experimental.pallas import tpu as pltpu
from jax.sharding import Mesh, PartitionSpec as P


HD = 64
PWIN = 8
WINDOW = 512
HALO = 32
EPS = 1e-05
QROWS = 256
BROWS = 512

NZ, NY, NX, NC = 8, 4, 4, 2
NF = NX * NC
SEQ = ("z", "y")
FFN = ("x", "c")
BF = jnp.bfloat16
F32 = jnp.float32

UP = [(i, (i + 1) % 4) for i in range(4)]
DOWN = [(i, (i - 1) % 4) for i in range(4)]
ACROSS = [(i, (i + 2) % 4) for i in range(4)]
SCALE = 1.0 / math.sqrt(HD)


def sds(shape, dtype):
    return jax.ShapeDtypeStruct(shape, dtype)


def smem(*scalars):
    return jnp.stack([s.astype(jnp.int32) for s in scalars])


def cost(micros):
    return pl.CostEstimate(
        flops=int(micros * 6e8), transcendentals=0, bytes_accessed=int(micros * 2.5e6)
    )


def call(kernel, out, *args, micros=4, scalars=None, anywhere=(), scratch=()):
    offset = 0 if scalars is None else 1
    specs = [
        pl.BlockSpec(memory_space=pl.ANY if i in anywhere else pltpu.VMEM)
        for i in range(len(args))
    ]
    if offset:
        specs = [pl.BlockSpec(memory_space=pltpu.SMEM)] + specs
        args = (scalars,) + args
    return pl.pallas_call(
        kernel,
        out_shape=out,
        in_specs=specs,
        out_specs=jax.tree.map(lambda _: pl.BlockSpec(memory_space=pltpu.VMEM), out),
        scratch_shapes=list(scratch),
        cost_estimate=cost(micros),
    )(*args)


def swap(value, axes):
    return lax.all_to_all(value, axes, split_axis=0, concat_axis=0, tiled=True)


def ring(value, axis):
    half = value.shape[0] // 2
    before = lax.ppermute(value, axis, UP)
    after = lax.ppermute(value, axis, DOWN)
    far_low = lax.ppermute(before[:half], axis, UP)
    far_high = lax.ppermute(after[half:], axis, DOWN)
    return before, after, far_low, far_high


def other_core(value):
    return lax.ppermute(value, "c", [(0, 1), (1, 0)])


def dot(a, b):
    return jnp.dot(a, b, preferred_element_type=F32)


def dot_nt(a, b):
    return lax.dot_general(a, b, (((1,), (1,)), ((), ())), preferred_element_type=F32)


def norm_kernel(place, patches, _after, normed, half):
    wide = patches[...].astype(F32)
    mean = jnp.mean(wide * wide, axis=-1, keepdims=True)
    normed[...] = (wide * lax.rsqrt(mean + EPS)).astype(BF)
    half[...] = normed[pl.ds(pl.multiple_of(place[2] * half.shape[0], half.shape[0]), half.shape[0])]


def mix_kernel(place, down_t, *refs):
    out = refs[-1]
    x, core = place[0], place[2]
    lhs = jnp.concatenate([down_t[z] for z in range(NZ)], axis=1)
    for side in range(2):
        own, before, after, low, high = refs[5 * side : 5 * side + 5]
        at = core if side == 0 else 1 - core
        half = low.shape[0]
        out[NC * x + at] = dot(lhs, own[...])
        out[NC * ((x + 3) % NX) + at] = dot(lhs, before[...])
        out[NC * ((x + 1) % NX) + at] = dot(lhs, after[...])
        out[NC * ((x + 2) % NX) + at] = dot(lhs[:, :half], low[...]) + dot(
            lhs[:, half:], high[...]
        )


def mix_sum_kernel(terms, cross_out, self_out, mix, outs):
    total = terms[0]
    for i in range(1, NY):
        total = total + terms[i]
    total = total.astype(BF)
    for z in range(NZ):
        mix[z] = total
    rows = cross_out.shape[0]
    outs[:rows] = cross_out[...]
    outs[rows:] = self_out[...]


def project_kernel(states, w_qs, w_qc, w_k, w_v, qs, qc, kv):
    first = dot(states[...], jnp.concatenate([w_qs[...], w_qc[...]], axis=1)).astype(BF)
    cols = qs.shape[1]
    qs[...] = first[:, :cols]
    qc[...] = first[:, cols:]
    kv[...] = dot(states[...], jnp.concatenate([w_k[...], w_v[...]], axis=1)).astype(BF)


def project(states, w_qs, w_qc, w_k, w_v):
    count, width = states.shape
    cols = w_qs.shape[1]
    weight = pl.BlockSpec((width, cols), lambda i: (0, 0))
    narrow = pl.BlockSpec((BROWS, cols), lambda i: (i, 0))
    return pl.pallas_call(
        project_kernel,
        out_shape=(sds((count, cols), BF), sds((count, cols), BF), sds((count, 2 * cols), BF)),
        grid=(count // BROWS,),
        in_specs=[pl.BlockSpec((BROWS, width), lambda i: (i, 0))] + [weight] * 4,
        out_specs=(narrow, narrow, pl.BlockSpec((BROWS, 2 * cols), lambda i: (i, 0))),
        cost_estimate=cost(6),
    )(states, w_qs, w_qc, w_k, w_v)


def window_kernel(base, place, query, kv, before, out, stacked):
    step = pl.program_id(0) + base
    cols = query.shape[1]

    @pl.when(step == base)
    def _():
        stacked[:WINDOW] = before[...]
        stacked[WINDOW:] = kv[...]

    count = kv.shape[0]
    first = WINDOW - place[3] * count - step * QROWS
    row = lax.broadcasted_iota(jnp.int32, (QROWS, QROWS), 0)
    col = lax.broadcasted_iota(jnp.int32, (QROWS, QROWS), 1)
    tiles = WINDOW // QROWS + 1
    start = pl.multiple_of(step * QROWS, QROWS)
    for head in range(cols // HD):
        lanes = slice(head * HD, (head + 1) * HD)
        q = query[:, lanes] * SCALE
        scores = []
        for t in range(tiles):
            keys = stacked[pl.ds(start + t * QROWS, QROWS), lanes]
            s = dot_nt(q, keys)
            if t == 0:
                s = jnp.where((col > row) & (col >= first), s, -jnp.inf)
            elif t < tiles - 1:
                s = jnp.where(col >= first - t * QROWS, s, -jnp.inf)
            else:
                s = jnp.where(col <= row, s, -jnp.inf)
            scores.append(s)
        s = jnp.concatenate(scores, axis=1)
        e = jnp.exp(s - jnp.max(s, axis=-1, keepdims=True))
        w = (e * (1.0 / jnp.sum(e, axis=-1, keepdims=True))).astype(BF)
        values = stacked[
            pl.ds(start, tiles * QROWS), cols + head * HD : cols + (head + 1) * HD
        ]
        out[:, lanes] = dot(w, values).astype(BF)


def window_attention(place, query, kv, before, part):
    count, cols = query.shape
    steps = count // QROWS // 2
    first = part * steps
    block = pl.BlockSpec((QROWS, cols), lambda i: (i, 0))
    return pl.pallas_call(
        functools.partial(window_kernel, first),
        out_shape=sds((count // 2, cols), BF),
        grid=(steps,),
        in_specs=[
            pl.BlockSpec(memory_space=pltpu.SMEM),
            pl.BlockSpec((QROWS, cols), lambda i: (i + first, 0)),
            pl.BlockSpec(kv.shape, lambda i: (0, 0)),
            pl.BlockSpec(before.shape, lambda i: (0, 0)),
        ],
        out_specs=block,
        scratch_shapes=[pltpu.VMEM((WINDOW + count, 2 * cols), BF)],
        cost_estimate=cost(7),
    )(place, query, kv, before)


def ffn_kernel(place, *refs):
    pieces, gate_up = refs[:9], refs[9]
    outs = refs[10:14]
    rows_buf, weight_buf, sems = refs[14:]
    core = place[2]
    rows = pieces[0].shape[0]
    half, quarter = rows // 2, rows // 4
    own, other = core * half, (1 - core) * half
    starts = [0]
    for slab in (1, 2):
        starts += [slab * rows + own, slab * rows + other]
    starts += [3 * rows + own, 3 * rows + own + quarter]
    starts += [3 * rows + other, 3 * rows + other + quarter]
    weight_copy = pltpu.make_async_copy(gate_up, weight_buf, sems.at[9])
    weight_copy.start()
    copies = []
    for i, piece in enumerate(pieces):
        size = piece.shape[0]
        at = pl.multiple_of(starts[i], quarter)
        copies.append(pltpu.make_async_copy(piece, rows_buf.at[pl.ds(at, size)], sems.at[i]))
        copies[-1].start()
    slot = outs[0].shape[1]
    weight_copy.wait()
    for slab, used in enumerate(((0,), (1, 2), (3, 4), (5, 6, 7, 8))):
        for i in used:
            copies[i].wait()
        sums = dot(rows_buf[slab * rows : (slab + 1) * rows], weight_buf[...])
        gate = sums[:, :slot]
        outs[slab][...] = (gate * (1.0 / (1.0 + jnp.exp(-gate))) * sums[:, slot:]).astype(BF)


def part_kernel(place, own, after, before, far, m_own, m_after, m_before, m_low, m_high, out, hid):
    y = place[1]
    hid[y] = own[...]
    hid[(y + 1) % NY] = after[...]
    hid[(y + 3) % NY] = before[...]
    hid[(y + 2) % NY] = far[...]
    keep = 2 * m_own.shape[2]
    low = m_low.shape[0]

    def product(get):
        total = None
        for block in range(NY):
            piece = jnp.concatenate([get(2 * block), get(2 * block + 1)], axis=0)
            term = dot(hid[block, :, :keep], piece)
            total = term if total is None else total + term
        return total.astype(BF)

    for p in range(2):
        out[2 * y + p] = product(lambda z: m_own[z, p])
        out[2 * ((y + 1) % NY) + p] = product(lambda z: m_after[z, p])
        out[2 * ((y + 3) % NY) + p] = product(lambda z: m_before[z, p])
        out[2 * ((y + 2) % NY) + p] = product(
            lambda z: m_low[z, p] if z < low else m_high[z - low, p]
        )


def keys_kernel(parts, own, kv, head, tail):
    total = own[...]
    for i in range(NF):
        total = total + parts[i].astype(F32)
    total = total.astype(BF)
    kv[...] = total
    head[...] = total[:HALO]
    tail[...] = total[-HALO:]


def cross_kernel(place, query, byte_patch, kv, before, after, out, stacked):
    step = pl.program_id(0)
    rows, both = kv.shape
    cols = both // 2

    @pl.when(step == 0)
    def _():
        stacked[:HALO] = before[...]
        stacked[HALO : HALO + rows] = kv[...]
        stacked[HALO + rows :] = after[...]

    total = rows + 2 * HALO
    shape = (total, query.shape[0])
    index = lax.broadcasted_iota(jnp.int32, shape, 0) + (place[3] * rows - HALO)
    held = byte_patch[...]
    mask = (index <= held) & (index > held - PWIN) & (index >= 0)
    for head in range(cols // HD):
        q = query[:, head * HD : (head + 1) * HD] * SCALE
        s = dot_nt(stacked[:, head * HD : (head + 1) * HD], q)
        s = jnp.where(mask, s, -jnp.inf)
        e = jnp.exp(s - jnp.max(s, axis=0, keepdims=True))
        w = (e * (1.0 / jnp.sum(e, axis=0, keepdims=True))).astype(BF)
        values = stacked[:, cols + head * HD : cols + (head + 1) * HD]
        context = lax.dot_general(
            values, w, (((0,), (0,)), ((), ())), preferred_element_type=F32
        )
        out[:, head * HD : (head + 1) * HD] = context.T.astype(BF)


def cross_attention(place, query, byte_patch, kv, before, after):
    count, cols = query.shape
    block = pl.BlockSpec((BROWS, cols), lambda i: (i, 0))

    def whole(value):
        return pl.BlockSpec(value.shape, lambda i: (0, 0))

    return pl.pallas_call(
        cross_kernel,
        out_shape=sds((count, cols), BF),
        grid=(count // BROWS,),
        in_specs=[
            pl.BlockSpec(memory_space=pltpu.SMEM),
            block,
            pl.BlockSpec((1, BROWS), lambda i: (0, i)),
            whole(kv),
            whole(before),
            whole(after),
        ],
        out_specs=block,
        scratch_shapes=[pltpu.VMEM((kv.shape[0] + 2 * HALO, 2 * cols), BF)],
        cost_estimate=cost(6),
    )(place, query, byte_patch.reshape(1, count), kv, before, after)


def out_product(context, outs, which):
    both = outs.shape[0] // NF
    half = both // 2
    weight = jnp.concatenate(
        [outs[f * both + which * half : f * both + (which + 1) * half] for f in range(NF)], axis=0
    )
    return dot(jnp.concatenate([context[f] for f in range(NF)], axis=1), weight)


def self_part_kernel(context, outs, out):
    out[...] = out_product(context, outs, 1)


def update_kernel(context, outs, self_part, out):
    total = (self_part[...] + out_product(context, outs, 0)).astype(BF)
    cols = out.shape[2]
    for f in range(NF):
        out[f] = total[:, f * cols : (f + 1) * cols]


def local(
    patches,
    gate_weight,
    up_weight,
    down_weight,
    key_weight,
    value_weight,
    byte_states,
    byte_patch,
    cross_query,
    self_query,
    self_key,
    self_value,
    cross_out,
    self_out,
):
    x, y, core = (lax.axis_index(a) for a in ("x", "y", "c"))
    place = smem(x, y, core, lax.axis_index(SEQ))
    rows, width = patches.shape
    d_rows, hid = gate_weight.shape
    hid_y = hid // NY
    hid_z = hid // NZ
    pad_y = -hid_y % 128
    slot = hid_y + pad_y
    head_cols = key_weight.shape[1]
    both_cols = 2 * head_cols
    byte_count = byte_states.shape[0]
    chunk = byte_count // NF

    def by_y(weight):
        pieces = weight.reshape(d_rows, NY, hid_y).transpose(1, 0, 2)
        return jnp.pad(pieces, ((0, 0), (0, 0), (0, pad_y)))

    gate_up = jnp.concatenate([by_y(gate_weight), by_y(up_weight)], axis=2)
    gate_up = swap(gate_up, "y")
    gate_up = gate_up.reshape(NY * d_rows, 2 * slot)

    def of_y(weight):
        grid = weight.reshape(NZ, NY, d_rows, head_cols)
        return lax.dynamic_slice_in_dim(grid, y, 1, axis=1)

    kv_rows = jnp.concatenate([of_y(key_weight), of_y(value_weight)], axis=3)
    kv_rows = kv_rows.reshape(NZ * d_rows, both_cols)
    kv_pieces = (kv_rows,) + ring(kv_rows, "x")
    kv_others = tuple(other_core(piece) for piece in kv_pieces)

    normed, own_half = call(
        norm_kernel,
        (sds((rows, width), BF), sds((rows // NC, width), BF)),
        patches,
        gate_up,
        scalars=place,
        anywhere=(1,),
    )
    gate_up = lax.all_gather(gate_up, "z", axis=0, tiled=True)
    down_t = swap(down_weight.T.reshape(NZ, hid_z, d_rows), "z")
    before, after, far_low, far_high = ring(own_half, "y")
    group = (
        normed,
        after,
        other_core(after),
        before,
        other_core(before),
        far_low,
        far_high,
        other_core(far_low),
        other_core(far_high),
    )

    mix = call(
        mix_kernel,
        sds((NF, hid_z, both_cols), F32),
        down_t,
        *kv_pieces,
        *kv_others,
        scalars=place,
    )
    mix = swap(mix.reshape(NY, NF // NY * hid_z, both_cols), "y")
    mix, outs = call(
        mix_sum_kernel,
        (
            sds((NZ, NF // NY * hid_z, both_cols), BF),
            sds((2 * head_cols, NF * head_cols), BF),
        ),
        mix,
        cross_out,
        self_out,
    )
    mix = swap(mix, "z").reshape(NZ, NF // NY, hid_z, both_cols)
    m_before, m_after, m_low, m_high = ring(mix, "y")
    outs = lax.all_gather(outs, FFN, axis=0, tiled=True)

    own_kv = dot(patches, key_weight), dot(patches, value_weight)
    own_kv = jnp.concatenate(own_kv, axis=1)

    query_s, query_c, both_s = project(byte_states, self_query, cross_query, self_key, self_value)
    steps = [(i, i + 1) for i in range(NZ * NY - 1)]
    back = [(j, i) for i, j in steps]
    tail = lax.ppermute(both_s[byte_count - WINDOW :], SEQ, steps)
    halves = []
    for half in range(2):
        halves.append(window_attention(place, query_s, both_s, tail, half))
    context_s = jnp.concatenate(halves).reshape(NF, chunk, head_cols)
    context_s = swap(context_s, FFN)
    self_part = call(self_part_kernel, sds((chunk, NF * head_cols), F32), context_s, outs)
    piece = sds((rows, slot), BF)
    h_own, h_after, h_before, h_far = call(
        ffn_kernel,
        (piece,) * 4,
        *group,
        gate_up,
        scalars=place,
        anywhere=range(10),
        scratch=(
            pltpu.VMEM((NY * rows, width), BF),
            pltpu.VMEM(gate_up.shape, BF),
            pltpu.SemaphoreType.DMA((10,)),
        ),
    )
    hid_after = lax.ppermute(h_before, "y", DOWN)
    hid_before = lax.ppermute(h_after, "y", UP)
    hid_far = lax.ppermute(h_far, "y", ACROSS)
    part = call(
        part_kernel,
        sds((NF, rows, both_cols), BF),
        h_own,
        hid_after,
        hid_before,
        hid_far,
        mix,
        m_after,
        m_before,
        m_low,
        m_high,
        scalars=place,
        scratch=(pltpu.VMEM((NY, rows, slot), BF),),
    )
    part = swap(part, FFN)
    both_c, head_rows, tail_rows = call(
        keys_kernel,
        (sds((rows, both_cols), BF),) + (sds((HALO, both_cols), BF),) * 2,
        part,
        own_kv,
    )
    context_c = cross_attention(
        place,
        query_c,
        byte_patch,
        both_c,
        lax.ppermute(tail_rows, SEQ, steps),
        lax.ppermute(head_rows, SEQ, back),
    )
    context_c = swap(context_c.reshape(NF, chunk, head_cols), FFN)
    update = call(
        update_kernel, sds((NF, chunk, head_cols), BF), context_c, outs, self_part
    )
    return swap(update, FFN).reshape(byte_count, head_cols)


def solution(mesh):
    fine = Mesh(mesh.devices.reshape(NZ, NY, NX, NC), SEQ + FFN)
    placed = (
        P(SEQ, None),
        P(SEQ, FFN),
        P(SEQ, FFN),
        P(SEQ, FFN),
        P(None, FFN),
        P(None, FFN),
        P(SEQ, None),
        P(SEQ),
        P(None, FFN),
        P(None, FFN),
        P(None, FFN),
        P(None, FFN),
        P(FFN, None),
        P(FFN, None),
    )
    return jax.shard_map(
        local, mesh=fine, in_specs=placed, out_specs=P(SEQ, FFN), check_vma=False
    )
```

```python
import functools
import math

import jax
import jax.numpy as jnp
from jax import lax
from jax.experimental import pallas as pl
from jax.experimental.pallas import tpu as pltpu
from jax.sharding import Mesh, PartitionSpec as P


HD = 64
PWIN = 8
WINDOW = 512
HALO = 32
EPS = 1e-05
QROWS = 256
BROWS = 512

NZ, NY, NX, NC = 8, 4, 4, 2
NF = NX * NC
SEQ = ("z", "y")
FFN = ("x", "c")
BF = jnp.bfloat16
F32 = jnp.float32

UP = [(i, (i + 1) % 4) for i in range(4)]
DOWN = [(i, (i - 1) % 4) for i in range(4)]
ACROSS = [(i, (i + 2) % 4) for i in range(4)]
SCALE = 1.0 / math.sqrt(HD)


def sds(shape, dtype):
    return jax.ShapeDtypeStruct(shape, dtype)


def smem(*scalars):
    return jnp.stack([s.astype(jnp.int32) for s in scalars])


def cost(micros):
    return pl.CostEstimate(
        flops=int(micros * 6e8), transcendentals=0, bytes_accessed=int(micros * 2.5e6)
    )


def call(kernel, out, *args, micros=4, scalars=None, anywhere=(), scratch=()):
    offset = 0 if scalars is None else 1
    specs = [
        pl.BlockSpec(memory_space=pl.ANY if i in anywhere else pltpu.VMEM)
        for i in range(len(args))
    ]
    if offset:
        specs = [pl.BlockSpec(memory_space=pltpu.SMEM)] + specs
        args = (scalars,) + args
    return pl.pallas_call(
        kernel,
        out_shape=out,
        in_specs=specs,
        out_specs=jax.tree.map(lambda _: pl.BlockSpec(memory_space=pltpu.VMEM), out),
        scratch_shapes=list(scratch),
        cost_estimate=cost(micros),
    )(*args)


def swap(value, axes):
    return lax.all_to_all(value, axes, split_axis=0, concat_axis=0, tiled=True)


def spread(value, axes, count):
    return swap(jnp.broadcast_to(value[None], (count,) + value.shape), axes)


def ring(value, axis):
    half = -(-value.shape[0] // 32) * 16
    before = lax.ppermute(value, axis, UP)
    after = lax.ppermute(value, axis, DOWN)
    far_low = lax.ppermute(before[:half], axis, UP)
    far_high = lax.ppermute(after[half:], axis, DOWN)
    return before, after, far_low, far_high


def other_core(value):
    return lax.ppermute(value, "c", [(0, 1), (1, 0)])


def dot(a, b):
    return jnp.dot(a, b, preferred_element_type=F32)


def dot_nt(a, b):
    return lax.dot_general(a, b, (((1,), (1,)), ((), ())), preferred_element_type=F32)


def norm_kernel(place, patches, _after, normed, half):
    wide = patches[...].astype(F32)
    mean = jnp.mean(wide * wide, axis=-1, keepdims=True)
    normed[...] = (wide * lax.rsqrt(mean + EPS)).astype(BF)
    half[...] = normed[pl.ds(pl.multiple_of(place[2] * half.shape[0], half.shape[0]), half.shape[0])]


def mix_kernel(place, down_t, *refs):
    out = refs[-1]
    x, core = place[0], place[2]
    lhs = jnp.concatenate([down_t[z] for z in range(NZ)], axis=1)
    cols = refs[0].shape[1]

    def store(at, value):
        out[:, pl.ds(pl.multiple_of(at * cols, cols), cols)] = value.astype(BF)

    for side in range(2):
        own, before, after, low, high = refs[5 * side : 5 * side + 5]
        at = core if side == 0 else 1 - core
        half = low.shape[0]
        store(NC * x + at, dot(lhs, own[...]))
        store(NC * ((x + 3) % NX) + at, dot(lhs, before[...]))
        store(NC * ((x + 1) % NX) + at, dot(lhs, after[...]))
        far = dot(lhs[:, :half], low[...]) + dot(lhs[:, half:], high[...])
        store(NC * ((x + 2) % NX) + at, far)


def mix_sum_kernel(own, before, after, low, high, mix):
    half = low.shape[0]
    near = own[...].astype(F32) + before[...].astype(F32) + after[...].astype(F32)
    mix[:half] = (near[:half] + low[...].astype(F32)).astype(BF)
    mix[half:] = (near[half:] + high[...].astype(F32)).astype(BF)


def project_kernel(states, w_qs, w_qc, w_k, w_v, qs, qc, kv):
    first = dot(states[...], jnp.concatenate([w_qs[...], w_qc[...]], axis=1)).astype(BF)
    cols = qs.shape[1]
    qs[...] = first[:, :cols]
    qc[...] = first[:, cols:]
    kv[...] = dot(states[...], jnp.concatenate([w_k[...], w_v[...]], axis=1)).astype(BF)


def project(states, w_qs, w_qc, w_k, w_v):
    count, width = states.shape
    cols = w_qs.shape[1]
    weight = pl.BlockSpec((width, cols), lambda i: (0, 0))
    narrow = pl.BlockSpec((BROWS, cols), lambda i: (i, 0))
    return pl.pallas_call(
        project_kernel,
        out_shape=(sds((count, cols), BF), sds((count, cols), BF), sds((count, 2 * cols), BF)),
        grid=(count // BROWS,),
        in_specs=[pl.BlockSpec((BROWS, width), lambda i: (i, 0))] + [weight] * 4,
        out_specs=(narrow, narrow, pl.BlockSpec((BROWS, 2 * cols), lambda i: (i, 0))),
        cost_estimate=cost(6),
    )(states, w_qs, w_qc, w_k, w_v)


def window_kernel(base, place, query, kv, before, out, stacked):
    step = pl.program_id(0) + base
    cols = query.shape[1]

    @pl.when(step == base)
    def _():
        stacked[:WINDOW] = before[...]
        stacked[WINDOW:] = kv[...]

    count = kv.shape[0]
    first = WINDOW - place[3] * count - step * QROWS
    row = lax.broadcasted_iota(jnp.int32, (QROWS, QROWS), 0)
    col = lax.broadcasted_iota(jnp.int32, (QROWS, QROWS), 1)
    tiles = WINDOW // QROWS + 1
    start = pl.multiple_of(step * QROWS, QROWS)
    for head in range(cols // HD):
        lanes = slice(head * HD, (head + 1) * HD)
        q = query[:, lanes] * SCALE
        scores = []
        for t in range(tiles):
            keys = stacked[pl.ds(start + t * QROWS, QROWS), lanes]
            s = dot_nt(q, keys)
            if t == 0:
                s = jnp.where((col > row) & (col >= first), s, -jnp.inf)
            elif t < tiles - 1:
                s = jnp.where(col >= first - t * QROWS, s, -jnp.inf)
            else:
                s = jnp.where(col <= row, s, -jnp.inf)
            scores.append(s)
        s = jnp.concatenate(scores, axis=1)
        e = jnp.exp(s - jnp.max(s, axis=-1, keepdims=True))
        w = (e * (1.0 / jnp.sum(e, axis=-1, keepdims=True))).astype(BF)
        values = stacked[
            pl.ds(start, tiles * QROWS), cols + head * HD : cols + (head + 1) * HD
        ]
        out[:, lanes] = dot(w, values).astype(BF)


def window_attention(place, query, kv, before, part):
    count, cols = query.shape
    steps = count // QROWS // 2
    first = part * steps
    block = pl.BlockSpec((QROWS, cols), lambda i: (i, 0))
    return pl.pallas_call(
        functools.partial(window_kernel, first),
        out_shape=sds((count // 2, cols), BF),
        grid=(steps,),
        in_specs=[
            pl.BlockSpec(memory_space=pltpu.SMEM),
            pl.BlockSpec((QROWS, cols), lambda i: (i + first, 0)),
            pl.BlockSpec(kv.shape, lambda i: (0, 0)),
            pl.BlockSpec(before.shape, lambda i: (0, 0)),
        ],
        out_specs=block,
        scratch_shapes=[pltpu.VMEM((WINDOW + count, 2 * cols), BF)],
        cost_estimate=cost(7),
    )(place, query, kv, before)


def ffn_kernel(place, *refs):
    pieces, gate_up = refs[:9], refs[9]
    outs = refs[10:14]
    rows_buf, weight_buf, sems = refs[14:]
    core = place[2]
    rows = pieces[0].shape[0]
    half, quarter = rows // 2, rows // 4
    own, other = core * half, (1 - core) * half
    starts = [0]
    for slab in (1, 2):
        starts += [slab * rows + own, slab * rows + other]
    starts += [3 * rows + own, 3 * rows + own + quarter]
    starts += [3 * rows + other, 3 * rows + other + quarter]
    weight_copy = pltpu.make_async_copy(gate_up, weight_buf, sems.at[9])
    weight_copy.start()
    copies = []
    for i, piece in enumerate(pieces):
        size = piece.shape[0]
        at = pl.multiple_of(starts[i], quarter)
        copies.append(pltpu.make_async_copy(piece, rows_buf.at[pl.ds(at, size)], sems.at[i]))
        copies[-1].start()
    slot = outs[0].shape[1]
    weight_copy.wait()
    for slab, used in enumerate(((0,), (1, 2), (3, 4), (5, 6, 7, 8))):
        for i in used:
            copies[i].wait()
        sums = dot(rows_buf[slab * rows : (slab + 1) * rows], weight_buf[...])
        gate = sums[:, :slot]
        outs[slab][...] = (gate * (1.0 / (1.0 + jnp.exp(-gate))) * sums[:, slot:]).astype(BF)


def edge_kernel(place, own, after, before, far, head, tail):
    y = place[1]
    for step, ref in enumerate((own, after, far, before)):
        head[(y + step) % NY] = ref[:HALO]
        tail[(y + step) % NY] = ref[-HALO:]


def part_kernel(place, own, after, before, far, above, below, mix, out, hid):
    y = place[1]
    rows = own.shape[0]
    for step, ref in enumerate((own, after, far, before)):
        hid[(y + step) % NY, HALO : HALO + rows] = ref[...]
    hid[:, :HALO] = above[...]
    hid[:, HALO + rows :] = below[...]
    keep = mix.shape[0] // NY
    cols = out.shape[2]
    for f in range(NF):
        total = None
        for block in range(NY):
            piece = mix[block * keep : (block + 1) * keep, f * cols : (f + 1) * cols]
            term = dot(hid[block, :, :keep], piece)
            total = term if total is None else total + term
        out[f] = total.astype(BF)


def keys_kernel(parts, own, above, below, kv):
    total = jnp.concatenate([above[...], own[...], below[...]], axis=0)
    for i in range(NF):
        total = total + parts[i].astype(F32)
    kv[...] = total.astype(BF)


def cross_kernel(place, query, byte_patch, stacked, out):
    total, both = stacked.shape
    cols = both // 2
    rows = total - 2 * HALO
    shape = (total, query.shape[0])
    index = lax.broadcasted_iota(jnp.int32, shape, 0) + (place[3] * rows - HALO)
    held = byte_patch[...]
    mask = (index <= held) & (index > held - PWIN) & (index >= 0)
    for head in range(cols // HD):
        q = query[:, head * HD : (head + 1) * HD] * SCALE
        s = dot_nt(stacked[:, head * HD : (head + 1) * HD], q)
        s = jnp.where(mask, s, -jnp.inf)
        e = jnp.exp(s - jnp.max(s, axis=0, keepdims=True))
        w = (e * (1.0 / jnp.sum(e, axis=0, keepdims=True))).astype(BF)
        values = stacked[:, cols + head * HD : cols + (head + 1) * HD]
        context = lax.dot_general(
            values, w, (((0,), (0,)), ((), ())), preferred_element_type=F32
        )
        out[:, head * HD : (head + 1) * HD] = context.T.astype(BF)


def cross_attention(place, query, byte_patch, kv):
    count, cols = query.shape
    block = pl.BlockSpec((BROWS, cols), lambda i: (i, 0))
    return pl.pallas_call(
        cross_kernel,
        out_shape=sds((count, cols), BF),
        grid=(count // BROWS,),
        in_specs=[
            pl.BlockSpec(memory_space=pltpu.SMEM),
            block,
            pl.BlockSpec((1, BROWS), lambda i: (0, i)),
            pl.BlockSpec(kv.shape, lambda i: (0, 0)),
        ],
        out_specs=block,
        cost_estimate=cost(6),
    )(place, query, byte_patch.reshape(1, count), kv)


def out_product(context, outs, which):
    both = outs.shape[0] // NF
    half = both // 2
    weight = jnp.concatenate(
        [outs[f * both + which * half : f * both + (which + 1) * half] for f in range(NF)], axis=0
    )
    return dot(jnp.concatenate([context[f] for f in range(NF)], axis=1), weight)


def self_part_kernel(context, outs, out):
    out[...] = out_product(context, outs, 1)


def update_kernel(context, outs, self_part, out):
    total = (self_part[...] + out_product(context, outs, 0)).astype(BF)
    cols = out.shape[2]
    for f in range(NF):
        out[f] = total[:, f * cols : (f + 1) * cols]


def local(
    patches,
    gate_weight,
    up_weight,
    down_weight,
    key_weight,
    value_weight,
    byte_states,
    byte_patch,
    cross_query,
    self_query,
    self_key,
    self_value,
    cross_out,
    self_out,
):
    x, y, core = (lax.axis_index(a) for a in ("x", "y", "c"))
    place = smem(x, y, core, lax.axis_index(SEQ))
    rows, width = patches.shape
    d_rows, hid = gate_weight.shape
    hid_y = hid // NY
    hid_z = hid // NZ
    pad_y = -hid_y % 128
    slot = hid_y + pad_y
    head_cols = key_weight.shape[1]
    both_cols = 2 * head_cols
    byte_count = byte_states.shape[0]
    chunk = byte_count // NF

    def by_y(weight):
        pieces = weight.reshape(d_rows, NY, hid_y).transpose(1, 0, 2)
        return jnp.pad(pieces, ((0, 0), (0, 0), (0, pad_y)))

    gate_up = jnp.concatenate([by_y(gate_weight), by_y(up_weight)], axis=2)
    gate_up = swap(gate_up, "y")
    gate_up = gate_up.reshape(NY * d_rows, 2 * slot)

    def of_y(weight):
        grid = weight.reshape(NZ, NY, d_rows, head_cols)
        return lax.dynamic_slice_in_dim(grid, y, 1, axis=1)

    kv_rows = jnp.concatenate([of_y(key_weight), of_y(value_weight)], axis=3)
    kv_rows = kv_rows.reshape(NZ * d_rows, both_cols)
    kv_pieces = (kv_rows,) + ring(kv_rows, "x")
    kv_others = tuple(other_core(piece) for piece in kv_pieces)

    normed, own_half = call(
        norm_kernel,
        (sds((rows, width), BF), sds((rows // NC, width), BF)),
        patches,
        gate_up,
        scalars=place,
        anywhere=(1,),
    )
    gate_up = lax.all_gather(gate_up, "z", axis=0, tiled=True)
    down_t = swap(down_weight.T.reshape(NZ, hid_z, d_rows), "z")
    before, after, far_low, far_high = ring(own_half, "y")
    group = (
        normed,
        after,
        other_core(after),
        before,
        other_core(before),
        far_low,
        far_high,
        other_core(far_low),
        other_core(far_high),
    )

    mix = call(
        mix_kernel,
        sds((hid_z, NF * both_cols), BF),
        down_t,
        *kv_pieces,
        *kv_others,
        scalars=place,
    )
    mixes = ring(mix, "y")
    mix = call(mix_sum_kernel, sds(mix.shape, BF), mix, *mixes)
    mix = lax.all_gather(mix, "z", axis=0, tiled=True)
    outs = spread(jnp.concatenate([cross_out, self_out]), FFN, NF)
    outs = outs.reshape(NF * 2 * head_cols, NF * head_cols)

    steps = [(i, i + 1) for i in range(NZ * NY - 1)]
    back = [(j, i) for i, j in steps]
    own_kv = dot(patches, key_weight), dot(patches, value_weight)
    own_kv = jnp.concatenate(own_kv, axis=1)
    own_above = lax.ppermute(own_kv[-HALO:], SEQ, steps)
    own_below = lax.ppermute(own_kv[:HALO], SEQ, back)

    query_s, query_c, both_s = project(byte_states, self_query, cross_query, self_key, self_value)
    tail = lax.ppermute(both_s[byte_count - WINDOW :], SEQ, steps)
    halves = []
    for half in range(2):
        halves.append(window_attention(place, query_s, both_s, tail, half))
    context_s = jnp.concatenate(halves).reshape(NF, chunk, head_cols)
    context_s = swap(context_s, FFN)
    self_part = call(self_part_kernel, sds((chunk, NF * head_cols), F32), context_s, outs)
    piece = sds((rows, slot), BF)
    h_own, h_after, h_before, h_far = call(
        ffn_kernel,
        (piece,) * 4,
        *group,
        gate_up,
        scalars=place,
        anywhere=range(10),
        scratch=(
            pltpu.VMEM((NY * rows, width), BF),
            pltpu.VMEM(gate_up.shape, BF),
            pltpu.SemaphoreType.DMA((10,)),
        ),
    )
    hid_after = lax.ppermute(h_before, "y", DOWN)
    hid_before = lax.ppermute(h_after, "y", UP)
    hid_far = lax.ppermute(h_far, "y", ACROSS)
    edges = (sds((NY, HALO, slot), BF),) * 2
    head, tail = call(
        edge_kernel, edges, h_own, hid_after, hid_before, hid_far, micros=2, scalars=place
    )
    above = lax.ppermute(tail, SEQ, steps)
    below = lax.ppermute(head, SEQ, back)
    part = call(
        part_kernel,
        sds((NF, rows + 2 * HALO, both_cols), BF),
        h_own,
        hid_after,
        hid_before,
        hid_far,
        above,
        below,
        mix,
        scalars=place,
        scratch=(pltpu.VMEM((NY, rows + 2 * HALO, slot), BF),),
    )
    part = swap(part, FFN)
    both_c = call(
        keys_kernel,
        sds((rows + 2 * HALO, both_cols), BF),
        part,
        own_kv,
        own_above,
        own_below,
    )

    context_c = cross_attention(place, query_c, byte_patch, both_c)
    context_c = swap(context_c.reshape(NF, chunk, head_cols), FFN)
    update = call(
        update_kernel, sds((NF, chunk, head_cols), BF), context_c, outs, self_part
    )
    return swap(update, FFN).reshape(byte_count, head_cols)


def solution(mesh):
    fine = Mesh(mesh.devices.reshape(NZ, NY, NX, NC), SEQ + FFN)
    placed = (
        P(SEQ, None),
        P(SEQ, FFN),
        P(SEQ, FFN),
        P(SEQ, FFN),
        P(None, FFN),
        P(None, FFN),
        P(SEQ, None),
        P(SEQ),
        P(None, FFN),
        P(None, FFN),
        P(None, FFN),
        P(None, FFN),
        P(FFN, None),
        P(FFN, None),
    )
    return jax.shard_map(local, mesh=fine, in_specs=placed, out_specs=P(SEQ, FFN), check_vma=False)
```

```python
import math

import jax
import jax.numpy as jnp
from jax import lax
from jax.experimental import pallas as pl
from jax.experimental.pallas import tpu as pltpu
from jax.sharding import Mesh, PartitionSpec as P


HD = 64
PWIN = 8
WINDOW = 512
HALO = 32
EPS = 1e-05
QROWS = 256
BROWS = 512

NZ, NY, NX, NC = 8, 4, 4, 2
NF = NX * NC
SEQ = ("z", "y")
FFN = ("x", "c")
BF = jnp.bfloat16
F32 = jnp.float32

UP = [(i, (i + 1) % 4) for i in range(4)]
DOWN = [(i, (i - 1) % 4) for i in range(4)]
ACROSS = [(i, (i + 2) % 4) for i in range(4)]
SCALE = 1.0 / math.sqrt(HD)


def sds(shape, dtype):
    return jax.ShapeDtypeStruct(shape, dtype)


def smem(*scalars):
    return jnp.stack([s.astype(jnp.int32) for s in scalars])


def cost(micros):
    return pl.CostEstimate(
        flops=int(micros * 6e8), transcendentals=0, bytes_accessed=int(micros * 2.5e6)
    )


def call(kernel, out, *args, micros=4, scalars=None, anywhere=(), scratch=()):
    offset = 0 if scalars is None else 1
    specs = [
        pl.BlockSpec(memory_space=pl.ANY if i in anywhere else pltpu.VMEM)
        for i in range(len(args))
    ]
    if offset:
        specs = [pl.BlockSpec(memory_space=pltpu.SMEM)] + specs
        args = (scalars,) + args
    return pl.pallas_call(
        kernel,
        out_shape=out,
        in_specs=specs,
        out_specs=jax.tree.map(lambda _: pl.BlockSpec(memory_space=pltpu.VMEM), out),
        scratch_shapes=list(scratch),
        cost_estimate=cost(micros),
    )(*args)


def swap(value, axes):
    return lax.all_to_all(value, axes, split_axis=0, concat_axis=0, tiled=True)


def spread(value, axes, count):
    return swap(jnp.broadcast_to(value[None], (count,) + value.shape), axes)


def ring(value, axis):
    half = -(-value.shape[0] // 32) * 16
    before = lax.ppermute(value, axis, UP)
    after = lax.ppermute(value, axis, DOWN)
    far_low = lax.ppermute(before[:half], axis, UP)
    far_high = lax.ppermute(after[half:], axis, DOWN)
    return before, after, far_low, far_high


def other_core(value):
    return lax.ppermute(value, "c", [(0, 1), (1, 0)])


def dot(a, b):
    return jnp.dot(a, b, preferred_element_type=F32)


def dot_nt(a, b):
    return lax.dot_general(a, b, (((1,), (1,)), ((), ())), preferred_element_type=F32)


def norm_kernel(place, patches, normed, half):
    chunk = 32

    def body(i, carry):
        at = pl.ds(pl.multiple_of(i * chunk, chunk), chunk)
        wide = patches[at].astype(F32)
        mean = jnp.mean(wide * wide, axis=-1, keepdims=True)
        normed[at] = (wide * lax.rsqrt(mean + EPS)).astype(BF)
        return carry

    lax.fori_loop(0, patches.shape[0] // chunk, body, 0)
    half[...] = normed[pl.ds(pl.multiple_of(place[2] * half.shape[0], half.shape[0]), half.shape[0])]


def mix_kernel(place, down_t, *refs):
    out = refs[-1]
    x, core = place[0], place[2]
    lhs = jnp.concatenate([down_t[z] for z in range(NZ)], axis=1)
    cols = refs[0].shape[1]

    def store(at, value):
        out[:, pl.ds(pl.multiple_of(at * cols, cols), cols)] = value.astype(BF)

    for side in range(2):
        own, before, after, low, high = refs[5 * side : 5 * side + 5]
        at = core if side == 0 else 1 - core
        half = low.shape[0]
        store(NC * x + at, dot(lhs, own[...]))
        store(NC * ((x + 3) % NX) + at, dot(lhs, before[...]))
        store(NC * ((x + 1) % NX) + at, dot(lhs, after[...]))
        far = dot(lhs[:, :half], low[...]) + dot(lhs[:, half:], high[...])
        store(NC * ((x + 2) % NX) + at, far)


def mix_sum_kernel(own, before, after, low, high, mix):
    half = low.shape[0]
    near = own[...].astype(F32) + before[...].astype(F32) + after[...].astype(F32)
    mix[:half] = (near[:half] + low[...].astype(F32)).astype(BF)
    mix[half:] = (near[half:] + high[...].astype(F32)).astype(BF)


def project_kernel(states, w_qs, w_qc, w_k, w_v, qs, qc, kv):
    first = dot(states[...], jnp.concatenate([w_qs[...], w_qc[...]], axis=1)).astype(BF)
    cols = qs.shape[1]
    qs[...] = first[:, :cols]
    qc[...] = first[:, cols:]
    kv[...] = dot(states[...], jnp.concatenate([w_k[...], w_v[...]], axis=1)).astype(BF)


def project(states, w_qs, w_qc, w_k, w_v):
    count, width = states.shape
    cols = w_qs.shape[1]
    weight = pl.BlockSpec((width, cols), lambda i: (0, 0))
    narrow = pl.BlockSpec((BROWS, cols), lambda i: (i, 0))
    return pl.pallas_call(
        project_kernel,
        out_shape=(sds((count, cols), BF), sds((count, cols), BF), sds((count, 2 * cols), BF)),
        grid=(count // BROWS,),
        in_specs=[pl.BlockSpec((BROWS, width), lambda i: (i, 0))] + [weight] * 4,
        out_specs=(narrow, narrow, pl.BlockSpec((BROWS, 2 * cols), lambda i: (i, 0))),
        cost_estimate=cost(6),
    )(states, w_qs, w_qc, w_k, w_v)


def window_kernel(place, query, kv, before, out, stacked):
    step = pl.program_id(0)
    cols = query.shape[1]

    @pl.when(step == 0)
    def _():
        stacked[:WINDOW] = before[...]
        stacked[WINDOW:] = kv[...]

    count = kv.shape[0]
    first = WINDOW - place[3] * count - step * QROWS
    row = lax.broadcasted_iota(jnp.int32, (QROWS, QROWS), 0)
    col = lax.broadcasted_iota(jnp.int32, (QROWS, QROWS), 1)
    tiles = WINDOW // QROWS + 1
    start = pl.multiple_of(step * QROWS, QROWS)
    for head in range(cols // HD):
        lanes = slice(head * HD, (head + 1) * HD)
        q = query[:, lanes] * SCALE
        scores = []
        for t in range(tiles):
            keys = stacked[pl.ds(start + t * QROWS, QROWS), lanes]
            s = dot_nt(q, keys)
            if t == 0:
                s = jnp.where((col > row) & (col >= first), s, -jnp.inf)
            elif t < tiles - 1:
                s = jnp.where(col >= first - t * QROWS, s, -jnp.inf)
            else:
                s = jnp.where(col <= row, s, -jnp.inf)
            scores.append(s)
        s = jnp.concatenate(scores, axis=1)
        e = jnp.exp(s - jnp.max(s, axis=-1, keepdims=True))
        w = (e * (1.0 / jnp.sum(e, axis=-1, keepdims=True))).astype(BF)
        values = stacked[
            pl.ds(start, tiles * QROWS), cols + head * HD : cols + (head + 1) * HD
        ]
        out[:, lanes] = dot(w, values).astype(BF)


def window_attention(place, query, kv, before):
    count, cols = query.shape
    block = pl.BlockSpec((QROWS, cols), lambda i: (i, 0))
    return pl.pallas_call(
        window_kernel,
        out_shape=sds((count, cols), BF),
        grid=(count // QROWS,),
        in_specs=[
            pl.BlockSpec(memory_space=pltpu.SMEM),
            block,
            pl.BlockSpec(kv.shape, lambda i: (0, 0)),
            pl.BlockSpec(before.shape, lambda i: (0, 0)),
        ],
        out_specs=block,
        scratch_shapes=[pltpu.VMEM((WINDOW + count, 2 * cols), BF)],
        cost_estimate=cost(14),
    )(place, query, kv, before)


def ffn_kernel(place, *refs):
    pieces, gate_up = refs[:9], refs[9]
    outs = refs[10:14]
    rows_buf, weight_buf, hidden, sems = refs[14:]
    core = place[2]
    rows = pieces[0].shape[0]
    half, quarter = rows // 2, rows // 4
    own, other = core * half, (1 - core) * half
    starts = [0]
    for slab in (1, 2):
        starts += [slab * rows + own, slab * rows + other]
    starts += [3 * rows + own, 3 * rows + own + quarter]
    starts += [3 * rows + other, 3 * rows + other + quarter]
    weight_copy = pltpu.make_async_copy(gate_up, weight_buf, sems.at[NY])
    weight_copy.start()
    for start, slab, piece in zip(starts, (0, 1, 1, 2, 2, 3, 3, 3, 3), pieces):
        at = pl.multiple_of(start, quarter)
        target = rows_buf.at[pl.ds(at, piece.shape[0])]
        pltpu.make_async_copy(piece, target, sems.at[slab]).start()
    slot = outs[0].shape[1]
    weight_copy.wait()

    def body(slab, carry):
        view = rows_buf.at[pl.ds(pl.multiple_of(slab * rows, rows), rows)]
        pltpu.make_async_copy(view, view, sems.at[slab]).wait()
        sums = dot(view[...], weight_buf[...])
        gate = sums[:, :slot]
        hidden[slab] = (gate * (1.0 / (1.0 + jnp.exp(-gate))) * sums[:, slot:]).astype(BF)
        return carry

    lax.fori_loop(0, NY, body, 0)
    for slab in range(NY):
        outs[slab][...] = hidden[slab]


def edge_kernel(place, own, after, before, far, head, tail):
    y = place[1]
    for step, ref in enumerate((own, after, far, before)):
        head[(y + step) % NY] = ref[:HALO]
        tail[(y + step) % NY] = ref[-HALO:]


def part_kernel(place, own, after, before, far, above, below, mix, out, hid):
    y = place[1]
    rows = own.shape[0]
    for step, ref in enumerate((own, after, far, before)):
        hid[(y + step) % NY, HALO : HALO + rows] = ref[...]
    hid[:, :HALO] = above[...]
    hid[:, HALO + rows :] = below[...]
    keep = mix.shape[0] // NY
    cols = out.shape[2]

    def body(f, carry):
        lanes = pl.ds(pl.multiple_of(f * cols, cols), cols)
        total = None
        for block in range(NY):
            piece = mix[block * keep : (block + 1) * keep, lanes]
            term = dot(hid[block, :, :keep], piece)
            total = term if total is None else total + term
        out[f] = total.astype(BF)
        return carry

    lax.fori_loop(0, NF, body, 0)


def keys_kernel(parts, own, above, below, kv):
    total = jnp.concatenate([above[...], own[...], below[...]], axis=0)
    for i in range(NF):
        total = total + parts[i].astype(F32)
    kv[...] = total.astype(BF)


def cross_kernel(place, query, byte_patch, stacked, out):
    total, both = stacked.shape
    cols = both // 2
    rows = total - 2 * HALO
    shape = (total, query.shape[0])
    index = lax.broadcasted_iota(jnp.int32, shape, 0) + (place[3] * rows - HALO)
    held = byte_patch[...]
    mask = (index <= held) & (index > jnp.maximum(held - PWIN, -1))
    contexts = []
    for head in range(cols // HD):
        q = query[:, head * HD : (head + 1) * HD] * SCALE
        s = dot_nt(stacked[:, head * HD : (head + 1) * HD], q)
        s = jnp.where(mask, s, -jnp.inf)
        e = jnp.exp(s - jnp.max(s, axis=0, keepdims=True))
        w = (e * (1.0 / jnp.sum(e, axis=0, keepdims=True))).astype(BF)
        values = stacked[:, cols + head * HD : cols + (head + 1) * HD]
        context = lax.dot_general(
            values, w, (((0,), (0,)), ((), ())), preferred_element_type=F32
        )
        contexts.append(context)
    out[...] = jnp.concatenate(contexts, axis=0).T.astype(BF)


def cross_attention(place, query, byte_patch, kv):
    count, cols = query.shape
    block = pl.BlockSpec((BROWS, cols), lambda i: (i, 0))
    return pl.pallas_call(
        cross_kernel,
        out_shape=sds((count, cols), BF),
        grid=(count // BROWS,),
        in_specs=[
            pl.BlockSpec(memory_space=pltpu.SMEM),
            block,
            pl.BlockSpec((1, BROWS), lambda i: (0, i)),
            pl.BlockSpec(kv.shape, lambda i: (0, 0)),
        ],
        out_specs=block,
        cost_estimate=cost(6),
    )(place, query, byte_patch.reshape(1, count), kv)


def out_product(context, outs, which):
    both = outs.shape[0] // NF
    half = both // 2
    weight = jnp.concatenate(
        [outs[f * both + which * half : f * both + (which + 1) * half] for f in range(NF)], axis=0
    )
    return dot(jnp.concatenate([context[f] for f in range(NF)], axis=1), weight)


def self_part_kernel(context, outs, out):
    out[...] = out_product(context, outs, 1)


def update_kernel(context, outs, self_part, out):
    total = (self_part[...] + out_product(context, outs, 0)).astype(BF)
    cols = out.shape[2]
    for f in range(NF):
        out[f] = total[:, f * cols : (f + 1) * cols]


def local(
    patches,
    gate_weight,
    up_weight,
    down_weight,
    key_weight,
    value_weight,
    byte_states,
    byte_patch,
    cross_query,
    self_query,
    self_key,
    self_value,
    cross_out,
    self_out,
):
    x, y, core = (lax.axis_index(a) for a in ("x", "y", "c"))
    place = smem(x, y, core, lax.axis_index(SEQ))
    rows, width = patches.shape
    d_rows, hid = gate_weight.shape
    hid_y = hid // NY
    hid_z = hid // NZ
    pad_y = -hid_y % 128
    slot = hid_y + pad_y
    head_cols = key_weight.shape[1]
    both_cols = 2 * head_cols
    byte_count = byte_states.shape[0]
    chunk = byte_count // NF

    def by_y(weight):
        pieces = weight.reshape(d_rows, NY, hid_y).transpose(1, 0, 2)
        return jnp.pad(pieces, ((0, 0), (0, 0), (0, pad_y)))

    gate_up = jnp.concatenate([by_y(gate_weight), by_y(up_weight)], axis=2)
    gate_up = swap(gate_up, "y")
    gate_up = gate_up.reshape(NY * d_rows, 2 * slot)

    def of_y(weight):
        grid = weight.reshape(NZ, NY, d_rows, head_cols)
        return lax.dynamic_slice_in_dim(grid, y, 1, axis=1)

    kv_rows = jnp.concatenate([of_y(key_weight), of_y(value_weight)], axis=3)
    kv_rows = kv_rows.reshape(NZ * d_rows, both_cols)
    kv_pieces = (kv_rows,) + ring(kv_rows, "x")
    kv_others = tuple(other_core(piece) for piece in kv_pieces)

    normed, own_half = call(
        norm_kernel,
        (sds((rows, width), BF), sds((rows // NC, width), BF)),
        patches,
        scalars=place,
    )
    gate_up = lax.all_gather(gate_up, "z", axis=0, tiled=True)
    down_t = swap(down_weight.T.reshape(NZ, hid_z, d_rows), "z")
    before, after, far_low, far_high = ring(own_half, "y")
    group = (
        normed,
        after,
        other_core(after),
        before,
        other_core(before),
        far_low,
        far_high,
        other_core(far_low),
        other_core(far_high),
    )

    mix = call(
        mix_kernel,
        sds((hid_z, NF * both_cols), BF),
        down_t,
        *kv_pieces,
        *kv_others,
        scalars=place,
    )
    mixes = ring(mix, "y")
    mix = call(mix_sum_kernel, sds(mix.shape, BF), mix, *mixes)
    mix = lax.all_gather(mix, "z", axis=0, tiled=True)
    outs = spread(jnp.concatenate([cross_out, self_out]), FFN, NF)
    outs = outs.reshape(NF * 2 * head_cols, NF * head_cols)

    steps = [(i, i + 1) for i in range(NZ * NY - 1)]
    back = [(j, i) for i, j in steps]
    own_kv = dot(patches, key_weight), dot(patches, value_weight)
    own_kv = jnp.concatenate(own_kv, axis=1)
    own_above = lax.ppermute(own_kv[-HALO:], SEQ, steps)
    own_below = lax.ppermute(own_kv[:HALO], SEQ, back)

    query_s, query_c, both_s = project(byte_states, self_query, cross_query, self_key, self_value)
    tail = lax.ppermute(both_s[byte_count - WINDOW :], SEQ, steps)
    context_s = window_attention(place, query_s, both_s, tail)
    context_s = swap(context_s.reshape(NF, chunk, head_cols), FFN)
    self_part = call(self_part_kernel, sds((chunk, NF * head_cols), F32), context_s, outs)
    piece = sds((rows, slot), BF)
    h_own, h_after, h_before, h_far = call(
        ffn_kernel,
        (piece,) * 4,
        *group,
        gate_up,
        scalars=place,
        anywhere=range(10),
        scratch=(
            pltpu.VMEM((NY * rows, width), BF),
            pltpu.VMEM(gate_up.shape, BF),
            pltpu.VMEM((NY, rows, slot), BF), pltpu.SemaphoreType.DMA((NY + 1,)),
        ),
    )
    hid_after = lax.ppermute(h_before, "y", DOWN)
    hid_before = lax.ppermute(h_after, "y", UP)
    hid_far = lax.ppermute(h_far, "y", ACROSS)
    edges = (sds((NY, HALO, slot), BF),) * 2
    head, tail = call(
        edge_kernel, edges, h_own, hid_after, hid_before, hid_far, micros=2, scalars=place
    )
    above = lax.ppermute(tail, SEQ, steps)
    below = lax.ppermute(head, SEQ, back)
    part = call(
        part_kernel,
        sds((NF, rows + 2 * HALO, both_cols), BF),
        h_own,
        hid_after,
        hid_before,
        hid_far,
        above,
        below,
        mix,
        scalars=place,
        scratch=(pltpu.VMEM((NY, rows + 2 * HALO, slot), BF),),
    )
    part = swap(part, FFN)
    both_c = call(
        keys_kernel,
        sds((rows + 2 * HALO, both_cols), BF),
        part,
        own_kv,
        own_above,
        own_below,
    )

    context_c = cross_attention(place, query_c, byte_patch, both_c)
    context_c = swap(context_c.reshape(NF, chunk, head_cols), FFN)
    update = call(
        update_kernel, sds((NF, chunk, head_cols), BF), context_c, outs, self_part
    )
    return swap(update, FFN).reshape(byte_count, head_cols)


def solution(mesh):
    fine = Mesh(mesh.devices.reshape(NZ, NY, NX, NC), SEQ + FFN)
    placed = (
        P(SEQ, None),
        P(SEQ, FFN),
        P(SEQ, FFN),
        P(SEQ, FFN),
        P(None, FFN),
        P(None, FFN),
        P(SEQ, None),
        P(SEQ),
        P(None, FFN),
        P(None, FFN),
        P(None, FFN),
        P(None, FFN),
        P(FFN, None),
        P(FFN, None),
    )
    return jax.shard_map(
        local, mesh=fine, in_specs=placed, out_specs=P(SEQ, FFN), check_vma=False
    )
```

```python
import math

import jax
import jax.numpy as jnp
from jax import lax
from jax.experimental import pallas as pl
from jax.experimental.pallas import tpu as pltpu
from jax.sharding import Mesh, PartitionSpec as P


HD = 64
PWIN = 8
WINDOW = 512
HALO = 32
EPS = 1e-05
QROWS = 256
BROWS = 512

NZ, NY, NX, NC = 8, 4, 4, 2
NF = NX * NC
SEQ = ("z", "y")
FFN = ("x", "c")
BF = jnp.bfloat16
F32 = jnp.float32

UP = [(i, (i + 1) % 4) for i in range(4)]
DOWN = [(i, (i - 1) % 4) for i in range(4)]
ACROSS = [(i, (i + 2) % 4) for i in range(4)]
SCALE = 1.0 / math.sqrt(HD)


def sds(shape, dtype):
    return jax.ShapeDtypeStruct(shape, dtype)


def smem(*scalars):
    return jnp.stack([s.astype(jnp.int32) for s in scalars])


def cost(micros):
    return pl.CostEstimate(
        flops=int(micros * 6e8), transcendentals=0, bytes_accessed=int(micros * 2.5e6)
    )


def call(kernel, out, *args, micros=4, scalars=None, anywhere=(), scratch=()):
    offset = 0 if scalars is None else 1
    specs = [
        pl.BlockSpec(memory_space=pl.ANY if i in anywhere else pltpu.VMEM)
        for i in range(len(args))
    ]
    if offset:
        specs = [pl.BlockSpec(memory_space=pltpu.SMEM)] + specs
        args = (scalars,) + args
    return pl.pallas_call(
        kernel,
        out_shape=out,
        in_specs=specs,
        out_specs=jax.tree.map(lambda _: pl.BlockSpec(memory_space=pltpu.VMEM), out),
        scratch_shapes=list(scratch),
        cost_estimate=cost(micros),
    )(*args)


def swap(value, axes):
    return lax.all_to_all(value, axes, split_axis=0, concat_axis=0, tiled=True)


def spread(value, axes, count):
    return swap(jnp.broadcast_to(value[None], (count,) + value.shape), axes)


def ring(value, axis):
    half = -(-value.shape[0] // 32) * 16
    before = lax.ppermute(value, axis, UP)
    after = lax.ppermute(value, axis, DOWN)
    far_low = lax.ppermute(before[:half], axis, UP)
    far_high = lax.ppermute(after[half:], axis, DOWN)
    return before, after, far_low, far_high


def other_core(value):
    return lax.ppermute(value, "c", [(0, 1), (1, 0)])


def dot(a, b):
    return jnp.dot(a, b, preferred_element_type=F32)


def dot_nt(a, b):
    return lax.dot_general(a, b, (((1,), (1,)), ((), ())), preferred_element_type=F32)


def norm_kernel(place, patches, normed, half):
    chunk = 32

    def body(i, carry):
        at = pl.ds(pl.multiple_of(i * chunk, chunk), chunk)
        wide = patches[at].astype(F32)
        mean = jnp.mean(wide * wide, axis=-1, keepdims=True)
        normed[at] = (wide * lax.rsqrt(mean + EPS)).astype(BF)
        return carry

    lax.fori_loop(0, patches.shape[0] // chunk, body, 0)
    half[...] = normed[pl.ds(pl.multiple_of(place[2] * half.shape[0], half.shape[0]), half.shape[0])]


def mix_kernel(place, down_t, *refs):
    out = refs[-1]
    x, core = place[0], place[2]
    lhs = jnp.concatenate([down_t[z] for z in range(NZ)], axis=1)
    cols = refs[0].shape[1]

    def store(at, value):
        out[:, pl.ds(pl.multiple_of(at * cols, cols), cols)] = value.astype(BF)

    for side in range(2):
        own, before, after, low, high = refs[5 * side : 5 * side + 5]
        at = core if side == 0 else 1 - core
        half = low.shape[0]
        store(NC * x + at, dot(lhs, own[...]))
        store(NC * ((x + 3) % NX) + at, dot(lhs, before[...]))
        store(NC * ((x + 1) % NX) + at, dot(lhs, after[...]))
        far = dot(lhs[:, :half], low[...]) + dot(lhs[:, half:], high[...])
        store(NC * ((x + 2) % NX) + at, far)


def mix_sum_kernel(own, before, after, low, high, mix):
    half = low.shape[0]
    near = own[...].astype(F32) + before[...].astype(F32) + after[...].astype(F32)
    mix[:half] = (near[:half] + low[...].astype(F32)).astype(BF)
    mix[half:] = (near[half:] + high[...].astype(F32)).astype(BF)


def project_kernel(states, w_qs, w_qc, w_k, w_v, qs, qc, kv):
    first = dot(states[...], jnp.concatenate([w_qs[...], w_qc[...]], axis=1)).astype(BF)
    cols = qs.shape[1]
    qs[...] = first[:, :cols]
    qc[...] = first[:, cols:]
    kv[...] = dot(states[...], jnp.concatenate([w_k[...], w_v[...]], axis=1)).astype(BF)


def project(states, w_qs, w_qc, w_k, w_v):
    count, width = states.shape
    cols = w_qs.shape[1]
    weight = pl.BlockSpec((width, cols), lambda i: (0, 0))
    narrow = pl.BlockSpec((BROWS, cols), lambda i: (i, 0))
    return pl.pallas_call(
        project_kernel,
        out_shape=(sds((count, cols), BF), sds((count, cols), BF), sds((count, 2 * cols), BF)),
        grid=(count // BROWS,),
        in_specs=[pl.BlockSpec((BROWS, width), lambda i: (i, 0))] + [weight] * 4,
        out_specs=(narrow, narrow, pl.BlockSpec((BROWS, 2 * cols), lambda i: (i, 0))),
        cost_estimate=cost(6),
    )(states, w_qs, w_qc, w_k, w_v)


def window_kernel(place, query, kv, before, out, stacked):
    step = pl.program_id(0)
    cols = query.shape[1]

    @pl.when(step == 0)
    def _():
        stacked[:WINDOW] = before[...]
        stacked[WINDOW:] = kv[...]

    count = kv.shape[0]
    first = WINDOW - place[3] * count - step * QROWS
    row = lax.broadcasted_iota(jnp.int32, (QROWS, QROWS), 0)
    col = lax.broadcasted_iota(jnp.int32, (QROWS, QROWS), 1)
    tiles = WINDOW // QROWS + 1
    start = pl.multiple_of(step * QROWS, QROWS)
    for head in range(cols // HD):
        lanes = slice(head * HD, (head + 1) * HD)
        q = query[:, lanes] * SCALE
        scores = []
        for t in range(tiles):
            keys = stacked[pl.ds(start + t * QROWS, QROWS), lanes]
            s = dot_nt(q, keys)
            if t == 0:
                s = jnp.where((col > row) & (col >= first), s, -jnp.inf)
            elif t < tiles - 1:
                s = jnp.where(col >= first - t * QROWS, s, -jnp.inf)
            else:
                s = jnp.where(col <= row, s, -jnp.inf)
            scores.append(s)
        s = jnp.concatenate(scores, axis=1)
        e = jnp.exp(s - jnp.max(s, axis=-1, keepdims=True))
        w = (e * (1.0 / jnp.sum(e, axis=-1, keepdims=True))).astype(BF)
        values = stacked[
            pl.ds(start, tiles * QROWS), cols + head * HD : cols + (head + 1) * HD
        ]
        out[:, lanes] = dot(w, values).astype(BF)


def window_attention(place, query, kv, before):
    count, cols = query.shape
    block = pl.BlockSpec((QROWS, cols), lambda i: (i, 0))
    return pl.pallas_call(
        window_kernel,
        out_shape=sds((count, cols), BF),
        grid=(count // QROWS,),
        in_specs=[
            pl.BlockSpec(memory_space=pltpu.SMEM),
            block,
            pl.BlockSpec(kv.shape, lambda i: (0, 0)),
            pl.BlockSpec(before.shape, lambda i: (0, 0)),
        ],
        out_specs=block,
        scratch_shapes=[pltpu.VMEM((WINDOW + count, 2 * cols), BF)],
        cost_estimate=cost(14),
    )(place, query, kv, before)


def ffn_kernel(place, *refs):
    pieces, gate_up = refs[:9], refs[9]
    outs = refs[10:14]
    rows_buf, weight_buf, hidden, sems = refs[14:]
    core = place[2]
    rows = pieces[0].shape[0]
    half, quarter = rows // 2, rows // 4
    own, other = core * half, (1 - core) * half
    starts = [0]
    for slab in (1, 2):
        starts += [slab * rows + own, slab * rows + other]
    starts += [3 * rows + own, 3 * rows + own + quarter]
    starts += [3 * rows + other, 3 * rows + other + quarter]
    weight_copy = pltpu.make_async_copy(gate_up, weight_buf, sems.at[NY])
    weight_copy.start()
    for start, slab, piece in zip(starts, (0, 1, 1, 2, 2, 3, 3, 3, 3), pieces):
        at = pl.multiple_of(start, quarter)
        target = rows_buf.at[pl.ds(at, piece.shape[0])]
        pltpu.make_async_copy(piece, target, sems.at[slab]).start()
    slot = outs[0].shape[1]
    weight_copy.wait()

    def body(slab, carry):
        view = rows_buf.at[pl.ds(pl.multiple_of(slab * rows, rows), rows)]
        pltpu.make_async_copy(view, view, sems.at[slab]).wait()
        sums = dot(view[...], weight_buf[...])
        gate = sums[:, :slot]
        hidden[slab] = (gate * (1.0 / (1.0 + jnp.exp(-gate))) * sums[:, slot:]).astype(BF)
        return carry

    lax.fori_loop(0, NY, body, 0)
    for slab in range(NY):
        outs[slab][...] = hidden[slab]


def edge_kernel(place, own, after, before, far, head, tail):
    y = place[1]
    for step, ref in enumerate((own, after, far, before)):
        head[(y + step) % NY] = ref[:HALO]
        tail[(y + step) % NY] = ref[-HALO:]


def part_kernel(place, own, after, before, far, above, below, mix, out, hid):
    y = place[1]
    rows = own.shape[0]
    for step, ref in enumerate((own, after, far, before)):
        hid[(y + step) % NY, HALO : HALO + rows] = ref[...]
    hid[:, :HALO] = above[...]
    hid[:, HALO + rows :] = below[...]
    keep = mix.shape[0] // NY
    cols = out.shape[2]

    def body(f, carry):
        lanes = pl.ds(pl.multiple_of(f * cols, cols), cols)
        total = None
        for block in range(NY):
            piece = mix[block * keep : (block + 1) * keep, lanes]
            term = dot(hid[block, :, :keep], piece)
            total = term if total is None else total + term
        out[f] = total.astype(BF)
        return carry

    lax.fori_loop(0, NF, body, 0)


def keys_kernel(parts, own, above, below, kv):
    total = jnp.concatenate([above[...], own[...], below[...]], axis=0)
    for i in range(NF):
        total = total + parts[i].astype(F32)
    kv[...] = total.astype(BF)


def cross_kernel(place, query, byte_patch, stacked, context_s, out):
    total, both = stacked.shape
    cols = both // 2
    rows = total - 2 * HALO
    shape = (total, query.shape[0])
    index = lax.broadcasted_iota(jnp.int32, shape, 0) + (place[3] * rows - HALO)
    held = byte_patch[...]
    mask = (index <= held) & (index > jnp.maximum(held - PWIN, -1))
    contexts = []
    for head in range(cols // HD):
        q = query[:, head * HD : (head + 1) * HD] * SCALE
        s = dot_nt(stacked[:, head * HD : (head + 1) * HD], q)
        s = jnp.where(mask, s, -jnp.inf)
        e = jnp.exp(s - jnp.max(s, axis=0, keepdims=True))
        w = (e * (1.0 / jnp.sum(e, axis=0, keepdims=True))).astype(BF)
        values = stacked[:, cols + head * HD : cols + (head + 1) * HD]
        context = lax.dot_general(
            values, w, (((0,), (0,)), ((), ())), preferred_element_type=F32
        )
        contexts.append(context)
    out[:, :cols] = jnp.concatenate(contexts, axis=0).T.astype(BF)
    out[:, cols:] = context_s[...]


def cross_attention(place, query, byte_patch, kv, context_s):
    count, cols = query.shape
    block = pl.BlockSpec((BROWS, cols), lambda i: (i, 0))
    return pl.pallas_call(
        cross_kernel,
        out_shape=sds((count, 2 * cols), BF),
        grid=(count // BROWS,),
        in_specs=[
            pl.BlockSpec(memory_space=pltpu.SMEM),
            block,
            pl.BlockSpec((1, BROWS), lambda i: (0, i)),
            pl.BlockSpec(kv.shape, lambda i: (0, 0)),
            block,
        ],
        out_specs=pl.BlockSpec((BROWS, 2 * cols), lambda i: (i, 0)),
        cost_estimate=cost(6),
    )(place, query, byte_patch.reshape(1, count), kv, context_s)


def update_kernel(context, outs, out):
    total = dot(jnp.concatenate([context[f] for f in range(NF)], axis=1), outs[...])
    total = total.astype(BF)
    cols = out.shape[2]
    for f in range(NF):
        out[f] = total[:, f * cols : (f + 1) * cols]


def local(
    patches,
    gate_weight,
    up_weight,
    down_weight,
    key_weight,
    value_weight,
    byte_states,
    byte_patch,
    cross_query,
    self_query,
    self_key,
    self_value,
    cross_out,
    self_out,
):
    x, y, core = (lax.axis_index(a) for a in ("x", "y", "c"))
    place = smem(x, y, core, lax.axis_index(SEQ))
    rows, width = patches.shape
    d_rows, hid = gate_weight.shape
    hid_y = hid // NY
    hid_z = hid // NZ
    pad_y = -hid_y % 128
    slot = hid_y + pad_y
    head_cols = key_weight.shape[1]
    both_cols = 2 * head_cols
    byte_count = byte_states.shape[0]
    chunk = byte_count // NF

    def by_y(weight):
        pieces = weight.reshape(d_rows, NY, hid_y).transpose(1, 0, 2)
        return jnp.pad(pieces, ((0, 0), (0, 0), (0, pad_y)))

    gate_up = jnp.concatenate([by_y(gate_weight), by_y(up_weight)], axis=2)
    gate_up = swap(gate_up, "y")
    gate_up = gate_up.reshape(NY * d_rows, 2 * slot)

    def of_y(weight):
        grid = weight.reshape(NZ, NY, d_rows, head_cols)
        return lax.dynamic_slice_in_dim(grid, y, 1, axis=1)

    kv_rows = jnp.concatenate([of_y(key_weight), of_y(value_weight)], axis=3)
    kv_rows = kv_rows.reshape(NZ * d_rows, both_cols)
    kv_pieces = (kv_rows,) + ring(kv_rows, "x")
    kv_others = tuple(other_core(piece) for piece in kv_pieces)

    normed, own_half = call(
        norm_kernel,
        (sds((rows, width), BF), sds((rows // NC, width), BF)),
        patches,
        scalars=place,
    )
    gate_up = lax.all_gather(gate_up, "z", axis=0, tiled=True)
    down_t = swap(down_weight.T.reshape(NZ, hid_z, d_rows), "z")
    before, after, far_low, far_high = ring(own_half, "y")
    group = (
        normed,
        after,
        other_core(after),
        before,
        other_core(before),
        far_low,
        far_high,
        other_core(far_low),
        other_core(far_high),
    )

    mix = call(
        mix_kernel,
        sds((hid_z, NF * both_cols), BF),
        down_t,
        *kv_pieces,
        *kv_others,
        scalars=place,
    )
    mixes = ring(mix, "y")
    mix = call(mix_sum_kernel, sds(mix.shape, BF), mix, *mixes)
    mix = lax.all_gather(mix, "z", axis=0, tiled=True)
    outs = spread(jnp.concatenate([cross_out, self_out]), FFN, NF)
    outs = outs.reshape(NF * 2 * head_cols, NF * head_cols)

    steps = [(i, i + 1) for i in range(NZ * NY - 1)]
    back = [(j, i) for i, j in steps]
    own_kv = dot(patches, key_weight), dot(patches, value_weight)
    own_kv = jnp.concatenate(own_kv, axis=1)
    own_above = lax.ppermute(own_kv[-HALO:], SEQ, steps)
    own_below = lax.ppermute(own_kv[:HALO], SEQ, back)

    query_s, query_c, both_s = project(byte_states, self_query, cross_query, self_key, self_value)
    tail = lax.ppermute(both_s[byte_count - WINDOW :], SEQ, steps)
    context_s = window_attention(place, query_s, both_s, tail)

    piece = sds((rows, slot), BF)
    h_own, h_after, h_before, h_far = call(
        ffn_kernel,
        (piece,) * 4,
        *group,
        gate_up,
        scalars=place,
        anywhere=range(10),
        scratch=(
            pltpu.VMEM((NY * rows, width), BF),
            pltpu.VMEM(gate_up.shape, BF),
            pltpu.VMEM((NY, rows, slot), BF), pltpu.SemaphoreType.DMA((NY + 1,)),
        ),
    )
    hid_after = lax.ppermute(h_before, "y", DOWN)
    hid_before = lax.ppermute(h_after, "y", UP)
    hid_far = lax.ppermute(h_far, "y", ACROSS)
    edges = (sds((NY, HALO, slot), BF),) * 2
    head, tail = call(
        edge_kernel, edges, h_own, hid_after, hid_before, hid_far, micros=2, scalars=place
    )
    above = lax.ppermute(tail, SEQ, steps)
    below = lax.ppermute(head, SEQ, back)
    part = call(
        part_kernel,
        sds((NF, rows + 2 * HALO, both_cols), BF),
        h_own,
        hid_after,
        hid_before,
        hid_far,
        above,
        below,
        mix,
        scalars=place,
        scratch=(pltpu.VMEM((NY, rows + 2 * HALO, slot), BF),),
    )
    part = swap(part, FFN)
    both_c = call(
        keys_kernel,
        sds((rows + 2 * HALO, both_cols), BF),
        part,
        own_kv,
        own_above,
        own_below,
    )

    context = cross_attention(place, query_c, byte_patch, both_c, context_s)
    context = swap(context.reshape(NF, chunk, both_cols), FFN)
    update = call(update_kernel, sds((NF, chunk, head_cols), BF), context, outs)
    return swap(update, FFN).reshape(byte_count, head_cols)


def solution(mesh):
    fine = Mesh(mesh.devices.reshape(NZ, NY, NX, NC), SEQ + FFN)
    placed = (
        P(SEQ, None),
        P(SEQ, FFN),
        P(SEQ, FFN),
        P(SEQ, FFN),
        P(None, FFN),
        P(None, FFN),
        P(SEQ, None),
        P(SEQ),
        P(None, FFN),
        P(None, FFN),
        P(None, FFN),
        P(None, FFN),
        P(FFN, None),
        P(FFN, None),
    )
    return jax.shard_map(
        local, mesh=fine, in_specs=placed, out_specs=P(SEQ, FFN), check_vma=False
    )
```

```python
import math

import jax
import jax.numpy as jnp
from jax import lax
from jax.experimental import pallas as pl
from jax.experimental.pallas import tpu as pltpu
from jax.sharding import Mesh, PartitionSpec as P


HD = 64
PWIN = 8
WINDOW = 512
HALO = 32
EPS = 1e-05
QROWS = 256
BROWS = 512

NZ, NY, NX, NC = 8, 4, 4, 2
NF = NX * NC
SEQ = ("z", "y")
FFN = ("x", "c")
BF = jnp.bfloat16
F32 = jnp.float32

UP = [(i, (i + 1) % 4) for i in range(4)]
DOWN = [(i, (i - 1) % 4) for i in range(4)]
ACROSS = [(i, (i + 2) % 4) for i in range(4)]
SCALE = 1.0 / math.sqrt(HD)


def sds(shape, dtype):
    return jax.ShapeDtypeStruct(shape, dtype)


def smem(*scalars):
    return jnp.stack([s.astype(jnp.int32) for s in scalars])


def cost(micros):
    return pl.CostEstimate(
        flops=int(micros * 6e8), transcendentals=0, bytes_accessed=int(micros * 2.5e6)
    )


def call(kernel, out, *args, micros=4, scalars=None, anywhere=(), scratch=()):
    offset = 0 if scalars is None else 1
    specs = [
        pl.BlockSpec(memory_space=pl.ANY if i in anywhere else pltpu.VMEM)
        for i in range(len(args))
    ]
    if offset:
        specs = [pl.BlockSpec(memory_space=pltpu.SMEM)] + specs
        args = (scalars,) + args
    return pl.pallas_call(
        kernel,
        out_shape=out,
        in_specs=specs,
        out_specs=jax.tree.map(lambda _: pl.BlockSpec(memory_space=pltpu.VMEM), out),
        scratch_shapes=list(scratch),
        cost_estimate=cost(micros),
    )(*args)


def swap(value, axes):
    return lax.all_to_all(value, axes, split_axis=0, concat_axis=0, tiled=True)


def spread(value, axes, count):
    return swap(jnp.broadcast_to(value[None], (count,) + value.shape), axes)


def ring(value, axis):
    half = -(-value.shape[0] // 32) * 16
    before = lax.ppermute(value, axis, UP)
    after = lax.ppermute(value, axis, DOWN)
    far_low = lax.ppermute(before[:half], axis, UP)
    far_high = lax.ppermute(after[half:], axis, DOWN)
    return before, after, far_low, far_high


def other_core(value):
    return lax.ppermute(value, "c", [(0, 1), (1, 0)])


def dot(a, b):
    return jnp.dot(a, b, preferred_element_type=F32)


def dot_nt(a, b):
    return lax.dot_general(a, b, (((1,), (1,)), ((), ())), preferred_element_type=F32)


def norm_kernel(place, patches, normed, half):
    chunk = 32

    def body(i, carry):
        at = pl.ds(pl.multiple_of(i * chunk, chunk), chunk)
        wide = patches[at].astype(F32)
        mean = jnp.mean(wide * wide, axis=-1, keepdims=True)
        normed[at] = (wide * lax.rsqrt(mean + EPS)).astype(BF)
        return carry

    lax.fori_loop(0, patches.shape[0] // chunk, body, 0)
    half[...] = normed[pl.ds(pl.multiple_of(place[2] * half.shape[0], half.shape[0]), half.shape[0])]


def mix_kernel(place, down_t, *refs):
    out = refs[-1]
    x, core = place[0], place[2]
    lhs = jnp.concatenate([down_t[z] for z in range(NZ)], axis=1)
    cols = refs[0].shape[1]

    def store(at, value):
        out[:, pl.ds(pl.multiple_of(at * cols, cols), cols)] = value.astype(BF)

    for side in range(2):
        own, before, after, low, high = refs[5 * side : 5 * side + 5]
        at = core if side == 0 else 1 - core
        half = low.shape[0]
        store(NC * x + at, dot(lhs, own[...]))
        store(NC * ((x + 3) % NX) + at, dot(lhs, before[...]))
        store(NC * ((x + 1) % NX) + at, dot(lhs, after[...]))
        far = dot(lhs[:, :half], low[...]) + dot(lhs[:, half:], high[...])
        store(NC * ((x + 2) % NX) + at, far)


def mix_sum_kernel(own, before, after, low, high, mix):
    half = low.shape[0]
    near = own[...].astype(F32) + before[...].astype(F32) + after[...].astype(F32)
    mix[:half] = (near[:half] + low[...].astype(F32)).astype(BF)
    mix[half:] = (near[half:] + high[...].astype(F32)).astype(BF)


def project_kernel(states, w_qs, w_qc, w_k, w_v, qs, qc, kv):
    first = dot(states[...], jnp.concatenate([w_qs[...], w_qc[...]], axis=1)).astype(BF)
    cols = qs.shape[1]
    qs[...] = first[:, :cols]
    qc[...] = first[:, cols:]
    kv[...] = dot(states[...], jnp.concatenate([w_k[...], w_v[...]], axis=1)).astype(BF)


def project(states, w_qs, w_qc, w_k, w_v):
    count, width = states.shape
    cols = w_qs.shape[1]
    weight = pl.BlockSpec((width, cols), lambda i: (0, 0))
    narrow = pl.BlockSpec((BROWS, cols), lambda i: (i, 0))
    return pl.pallas_call(
        project_kernel,
        out_shape=(sds((count, cols), BF), sds((count, cols), BF), sds((count, 2 * cols), BF)),
        grid=(count // BROWS,),
        in_specs=[pl.BlockSpec((BROWS, width), lambda i: (i, 0))] + [weight] * 4,
        out_specs=(narrow, narrow, pl.BlockSpec((BROWS, 2 * cols), lambda i: (i, 0))),
        cost_estimate=cost(6),
    )(states, w_qs, w_qc, w_k, w_v)


def window_kernel(place, query, kv, before, out, stacked):
    step = pl.program_id(0)
    cols = query.shape[1]

    @pl.when(step == 0)
    def _():
        stacked[:WINDOW] = before[...]
        stacked[WINDOW:] = kv[...]

    count = kv.shape[0]
    first = WINDOW - place[3] * count - step * QROWS
    row = lax.broadcasted_iota(jnp.int32, (QROWS, QROWS), 0)
    col = lax.broadcasted_iota(jnp.int32, (QROWS, QROWS), 1)
    tiles = WINDOW // QROWS + 1
    start = pl.multiple_of(step * QROWS, QROWS)
    for head in range(cols // HD):
        lanes = slice(head * HD, (head + 1) * HD)
        q = query[:, lanes] * SCALE
        scores = []
        for t in range(tiles):
            keys = stacked[pl.ds(start + t * QROWS, QROWS), lanes]
            s = dot_nt(q, keys)
            if t == 0:
                s = jnp.where((col > row) & (col >= first), s, -jnp.inf)
            elif t < tiles - 1:
                s = jnp.where(col >= first - t * QROWS, s, -jnp.inf)
            else:
                s = jnp.where(col <= row, s, -jnp.inf)
            scores.append(s)
        s = jnp.concatenate(scores, axis=1)
        e = jnp.exp(s - jnp.max(s, axis=-1, keepdims=True))
        w = (e * (1.0 / jnp.sum(e, axis=-1, keepdims=True))).astype(BF)
        values = stacked[
            pl.ds(start, tiles * QROWS), cols + head * HD : cols + (head + 1) * HD
        ]
        out[:, lanes] = dot(w, values).astype(BF)


def window_attention(place, query, kv, before):
    count, cols = query.shape
    block = pl.BlockSpec((QROWS, cols), lambda i: (i, 0))
    return pl.pallas_call(
        window_kernel,
        out_shape=sds((count, cols), BF),
        grid=(count // QROWS,),
        in_specs=[
            pl.BlockSpec(memory_space=pltpu.SMEM),
            block,
            pl.BlockSpec(kv.shape, lambda i: (0, 0)),
            pl.BlockSpec(before.shape, lambda i: (0, 0)),
        ],
        out_specs=block,
        scratch_shapes=[pltpu.VMEM((WINDOW + count, 2 * cols), BF)],
        cost_estimate=cost(14),
    )(place, query, kv, before)


def ffn_kernel(place, *refs):
    pieces, gate_up = refs[:9], refs[9]
    outs = refs[10:14]
    rows_buf, weight_buf, hidden, sems = refs[14:]
    core = place[2]
    rows = pieces[0].shape[0]
    half, quarter = rows // 2, rows // 4
    own, other = core * half, (1 - core) * half
    starts = [0]
    for slab in (1, 2):
        starts += [slab * rows + own, slab * rows + other]
    starts += [3 * rows + own, 3 * rows + own + quarter]
    starts += [3 * rows + other, 3 * rows + other + quarter]
    weight_copy = pltpu.make_async_copy(gate_up, weight_buf, sems.at[NY])
    weight_copy.start()
    for start, slab, piece in zip(starts, (0, 1, 1, 2, 2, 3, 3, 3, 3), pieces):
        at = pl.multiple_of(start, quarter)
        target = rows_buf.at[pl.ds(at, piece.shape[0])]
        pltpu.make_async_copy(piece, target, sems.at[slab]).start()
    slot = outs[0].shape[1]
    weight_copy.wait()

    def body(slab, carry):
        view = rows_buf.at[pl.ds(pl.multiple_of(slab * rows, rows), rows)]
        pltpu.make_async_copy(view, view, sems.at[slab]).wait()
        sums = dot(view[...], weight_buf[...])
        gate = sums[:, :slot]
        hidden[slab] = (gate * (1.0 / (1.0 + jnp.exp(-gate))) * sums[:, slot:]).astype(BF)
        return carry

    lax.fori_loop(0, NY, body, 0)
    for slab in range(NY):
        outs[slab][...] = hidden[slab]


def edge_kernel(place, own, after, before, far, head, tail):
    y = place[1]
    for step, ref in enumerate((own, after, far, before)):
        head[(y + step) % NY] = ref[:HALO]
        tail[(y + step) % NY] = ref[-HALO:]


def part_kernel(place, own, after, before, far, above, below, mix, out, hid):
    y = place[1]
    rows = own.shape[0]
    for step, ref in enumerate((own, after, far, before)):
        hid[(y + step) % NY, HALO : HALO + rows] = ref[...]
    hid[:, :HALO] = above[...]
    hid[:, HALO + rows :] = below[...]
    keep = mix.shape[0] // NY
    cols = out.shape[2]

    def body(f, carry):
        lanes = pl.ds(pl.multiple_of(f * cols, cols), cols)
        total = None
        for block in range(NY):
            piece = mix[block * keep : (block + 1) * keep, lanes]
            term = dot(hid[block, :, :keep], piece)
            total = term if total is None else total + term
        out[f] = total.astype(BF)
        return carry

    lax.fori_loop(0, NF, body, 0, unroll=True)


def cross_kernel(
    place, query, byte_patch, parts, own, above, below, context_s, out, stacked
):
    total, both = stacked.shape
    cols = both // 2
    rows = own.shape[0]

    @pl.when(pl.program_id(0) == 0)
    def _():
        sums = jnp.concatenate([above[...], own[...], below[...]], axis=0)
        for i in range(NF):
            sums = sums + parts[i].astype(F32)
        stacked[...] = sums.astype(BF)

    shape = (total, query.shape[0])
    index = lax.broadcasted_iota(jnp.int32, shape, 0) + (place[3] * rows - HALO)
    held = byte_patch[...]
    mask = (index <= held) & (index > jnp.maximum(held - PWIN, -1))
    contexts = []
    for head in range(cols // HD):
        q = query[:, head * HD : (head + 1) * HD] * SCALE
        s = dot_nt(stacked[:, head * HD : (head + 1) * HD], q)
        s = jnp.where(mask, s, -jnp.inf)
        e = jnp.exp(s - jnp.max(s, axis=0, keepdims=True))
        w = (e * (1.0 / jnp.sum(e, axis=0, keepdims=True))).astype(BF)
        values = stacked[:, cols + head * HD : cols + (head + 1) * HD]
        context = lax.dot_general(
            values, w, (((0,), (0,)), ((), ())), preferred_element_type=F32
        )
        contexts.append(context)
    out[:, :cols] = jnp.concatenate(contexts, axis=0).T.astype(BF)
    out[:, cols:] = context_s[...]


def cross_attention(place, query, byte_patch, parts, own, above, below, context_s):
    count, cols = query.shape

    def whole(value):
        return pl.BlockSpec(value.shape, lambda i: (0,) * value.ndim)

    block = pl.BlockSpec((BROWS, cols), lambda i: (i, 0))
    return pl.pallas_call(
        cross_kernel,
        out_shape=sds((count, 2 * cols), BF),
        grid=(count // BROWS,),
        in_specs=[
            pl.BlockSpec(memory_space=pltpu.SMEM),
            block,
            pl.BlockSpec((1, BROWS), lambda i: (0, i)),
            whole(parts),
            whole(own),
            whole(above),
            whole(below),
            block,
        ],
        out_specs=pl.BlockSpec((BROWS, 2 * cols), lambda i: (i, 0)),
        scratch_shapes=[pltpu.VMEM(parts.shape[1:], BF)],
        cost_estimate=cost(8),
    )(place, query, byte_patch.reshape(1, count), parts, own, above, below, context_s)


def update_kernel(context, outs, out):
    total = dot(jnp.concatenate([context[f] for f in range(NF)], axis=1), outs[...])
    total = total.astype(BF)
    cols = out.shape[2]
    for f in range(NF):
        out[f] = total[:, f * cols : (f + 1) * cols]


def local(
    patches,
    gate_weight,
    up_weight,
    down_weight,
    key_weight,
    value_weight,
    byte_states,
    byte_patch,
    cross_query,
    self_query,
    self_key,
    self_value,
    cross_out,
    self_out,
):
    x, y, core = (lax.axis_index(a) for a in ("x", "y", "c"))
    place = smem(x, y, core, lax.axis_index(SEQ))
    rows, width = patches.shape
    d_rows, hid = gate_weight.shape
    hid_y = hid // NY
    hid_z = hid // NZ
    pad_y = -hid_y % 128
    slot = hid_y + pad_y
    head_cols = key_weight.shape[1]
    both_cols = 2 * head_cols
    byte_count = byte_states.shape[0]
    chunk = byte_count // NF

    def by_y(weight):
        pieces = weight.reshape(d_rows, NY, hid_y).transpose(1, 0, 2)
        return jnp.pad(pieces, ((0, 0), (0, 0), (0, pad_y)))

    gate_up = jnp.concatenate([by_y(gate_weight), by_y(up_weight)], axis=2)
    gate_up = swap(gate_up, "y")
    gate_up = gate_up.reshape(NY * d_rows, 2 * slot)

    def of_y(weight):
        grid = weight.reshape(NZ, NY, d_rows, head_cols)
        return lax.dynamic_slice_in_dim(grid, y, 1, axis=1)

    kv_rows = jnp.concatenate([of_y(key_weight), of_y(value_weight)], axis=3)
    kv_rows = kv_rows.reshape(NZ * d_rows, both_cols)
    kv_pieces = (kv_rows,) + ring(kv_rows, "x")
    kv_others = tuple(other_core(piece) for piece in kv_pieces)

    normed, own_half = call(
        norm_kernel,
        (sds((rows, width), BF), sds((rows // NC, width), BF)),
        patches,
        scalars=place,
    )
    gate_up = lax.all_gather(gate_up, "z", axis=0, tiled=True)
    down_t = swap(down_weight.T.reshape(NZ, hid_z, d_rows), "z")
    before, after, far_low, far_high = ring(own_half, "y")
    group = (
        normed,
        after,
        other_core(after),
        before,
        other_core(before),
        far_low,
        far_high,
        other_core(far_low),
        other_core(far_high),
    )

    mix = call(
        mix_kernel,
        sds((hid_z, NF * both_cols), BF),
        down_t,
        *kv_pieces,
        *kv_others,
        scalars=place,
    )
    mixes = ring(mix, "y")
    mix = call(mix_sum_kernel, sds(mix.shape, BF), mix, *mixes)
    mix = lax.all_gather(mix, "z", axis=0, tiled=True)
    outs = spread(jnp.concatenate([cross_out, self_out]), FFN, NF)
    outs = outs.reshape(NF * 2 * head_cols, NF * head_cols)

    steps = [(i, i + 1) for i in range(NZ * NY - 1)]
    back = [(j, i) for i, j in steps]
    own_kv = dot(patches, key_weight), dot(patches, value_weight)
    own_kv = jnp.concatenate(own_kv, axis=1)
    own_above = lax.ppermute(own_kv[-HALO:], SEQ, steps)
    own_below = lax.ppermute(own_kv[:HALO], SEQ, back)

    query_s, query_c, both_s = project(byte_states, self_query, cross_query, self_key, self_value)
    tail = lax.ppermute(both_s[byte_count - WINDOW :], SEQ, steps)
    context_s = window_attention(place, query_s, both_s, tail)

    piece = sds((rows, slot), BF)
    h_own, h_after, h_before, h_far = call(
        ffn_kernel,
        (piece,) * 4,
        *group,
        gate_up,
        scalars=place,
        anywhere=range(10),
        scratch=(
            pltpu.VMEM((NY * rows, width), BF),
            pltpu.VMEM(gate_up.shape, BF),
            pltpu.VMEM((NY, rows, slot), BF), pltpu.SemaphoreType.DMA((NY + 1,)),
        ),
    )
    hid_after = lax.ppermute(h_before, "y", DOWN)
    hid_before = lax.ppermute(h_after, "y", UP)
    hid_far = lax.ppermute(h_far, "y", ACROSS)
    edges = (sds((NY, HALO, slot), BF),) * 2
    head, tail = call(
        edge_kernel, edges, h_own, hid_after, hid_before, hid_far, micros=2, scalars=place
    )
    above = lax.ppermute(tail, SEQ, steps)
    below = lax.ppermute(head, SEQ, back)
    part = call(
        part_kernel,
        sds((NF, rows + 2 * HALO, both_cols), BF),
        h_own,
        hid_after,
        hid_before,
        hid_far,
        above,
        below,
        mix,
        scalars=place,
        scratch=(pltpu.VMEM((NY, rows + 2 * HALO, slot), BF),),
    )
    part = swap(part, FFN)
    context = cross_attention(
        place, query_c, byte_patch, part, own_kv, own_above, own_below, context_s
    )
    context = swap(context.reshape(NF, chunk, both_cols), FFN)
    update = call(update_kernel, sds((NF, chunk, head_cols), BF), context, outs)
    return swap(update, FFN).reshape(byte_count, head_cols)


def solution(mesh):
    fine = Mesh(mesh.devices.reshape(NZ, NY, NX, NC), SEQ + FFN)
    placed = (
        P(SEQ, None),
        P(SEQ, FFN),
        P(SEQ, FFN),
        P(SEQ, FFN),
        P(None, FFN),
        P(None, FFN),
        P(SEQ, None),
        P(SEQ),
        P(None, FFN),
        P(None, FFN),
        P(None, FFN),
        P(None, FFN),
        P(FFN, None),
        P(FFN, None),
    )
    return jax.shard_map(
        local, mesh=fine, in_specs=placed, out_specs=P(SEQ, FFN), check_vma=False
    )
```
